128 devices in a mesh: grp: 4 (over y_hi, core), ctx: 32 (over x, y_lo, z).
Axes of the slice: x: 4, y: 4 (y_hi: 2, y_lo: 2; y = y_hi * 2 + y_lo), z: 4, core: 2. Of those that a mesh axis runs over, the one named last changes fastest.
Arguments:
- clip_queries: bfloat16 [4, 4096, 4096], P('grp', 'ctx'), may hold values from -6 to 6
- clip_keys: bfloat16 [4, 4096, 4096], P('grp', 'ctx'), may hold values from -6 to 6
- clip_values: bfloat16 [4, 4096, 4096], P('grp', 'ctx'), may hold values from -6 to 6
- cache_keys: bfloat16 [4, 4, 4096, 4096], P('grp', None, 'ctx'), may hold values from -6 to 6
- cache_values: bfloat16 [4, 4, 4096, 4096], P('grp', None, 'ctx'), may hold values from -6 to 6
- clip_pick: int32 [4, 2], P('grp'), may hold values from 0 to 3
- noisy_latent: bfloat16 [4, 128, 2, 1024], P('grp', 'ctx'), may hold values from -6 to 6
- prev_latent: bfloat16 [4, 128, 2, 1024], P('grp', 'ctx'), may hold values from -6 to 6
- velocity_weight: bfloat16 [4096, 64], replicated, may hold values from -0.09375 to 0.09375
- tile_owner: int32 [4, 128], P('grp', 'ctx'), may hold values from 0 to 3, as said below
- conv_in_weight: bfloat16 [432, 512], replicated, may hold values from -0.3125 to 0.3125
- conv_in_bias: float32 [512], replicated, may hold values from -4 to 4
- conv_out_weight: bfloat16 [9, 512, 128], replicated, may hold values from -0.09375 to 0.09375
- conv_out_bias: float32 [128], replicated, may hold values from -4 to 4
Outputs:
- decoded: bfloat16 [4, 32, 4, 2, 2, 256, 128], P('grp', 'ctx')
The draws below stay inside these ranges and needn't reach their ends.
Inputs may be any that keep to these rules, and one draw needn't show every extreme that they name: `tile_owner`: of one device's 4 tiles at most 2 name the same owner; in every draw some device names one owner 2 times, and some owner is named 2 times by every device with its ctx index.
All inputs are finite; a program needn't handle non-finite values.
Results may differ from the reference program's by a relative error of at most 0.007.
Values may be sent and summed in bfloat16 or wider, within the bound.
No kernel may reach another device: no remote copies, remote signals or barrier semaphores. Data moves between devices by JAX's collectives and lax.ppermute only.
A program may use at most 192 MiB of HBM per device.

```python
import math
import jax
import jax.numpy as jnp
from jax import lax

TILES_DEV = 4
LFR = 2
TP = 4
HEADS = 32
HD = 128
LAT = 16
DEC_MID = 512
DEC_OUT = 128
CACHE = 4
NCLIP = 4096
SLOT = 2
TL = 8
N_GRP = 4
N_CTX = 32


def draw_clip_queries(key, part):
    shape = (N_GRP, NCLIP, HEADS * HD)
    base = jnp.clip(jax.random.normal(jax.random.fold_in(key, 1), shape), -6.0, 6.0)
    return base.astype(jnp.bfloat16)


def draw_clip_keys(key, part):
    shape = (N_GRP, NCLIP, HEADS * HD)
    base = jnp.clip(jax.random.normal(jax.random.fold_in(key, 2), shape), -6.0, 6.0)
    return base.astype(jnp.bfloat16)


def column_scales(key):
    return jnp.exp(jax.random.uniform(jax.random.fold_in(key, 103), (HEADS * HD,), minval=math.log(0.3), maxval=math.log(3.0)))


def value_law(key, shape, salt):
    lead = shape[:-1] + (1,)
    base = jax.random.normal(jax.random.fold_in(key, salt), shape)
    row_scale = jnp.exp(jax.random.uniform(jax.random.fold_in(key, salt + 1), lead, minval=math.log(0.5), maxval=math.log(2.0)))
    values = base * column_scales(key) * row_scale
    return jnp.clip(values, -6.0, 6.0).astype(jnp.float32)


def draw_clip_values(key, part):
    return value_law(key, (N_GRP, NCLIP, HEADS * HD), 20).astype(jnp.bfloat16)


def draw_cache_values(key, part):
    return value_law(key, (N_GRP, CACHE, NCLIP, HEADS * HD), 30).astype(jnp.bfloat16)


def draw_tile_owner(key, part):
    devices_all = N_GRP * N_CTX
    split_keys = jax.random.split(jax.random.fold_in(key, 5), devices_all)
    perms = jax.vmap(lambda single: jax.random.permutation(single, N_GRP))(split_keys).reshape(N_GRP, N_CTX, N_GRP)
    modes = jax.random.randint(jax.random.fold_in(key, 6), (N_GRP, N_CTX), 0, 2)
    column = jax.random.randint(jax.random.fold_in(key, 7), (), 0, N_CTX)
    chosen = jax.random.randint(jax.random.fold_in(key, 8), (), 0, N_GRP)
    forced = (jnp.arange(N_CTX) == column)[None, :]
    shifted = (perms - perms[:, :, :1] + chosen) % N_GRP
    perms = jnp.where(forced[:, :, None], shifted, perms)
    modes = jnp.where(forced, 1, modes)
    tiles = jnp.arange(TILES_DEV)
    paired = jnp.take(perms, tiles // SLOT, axis=2)
    spread = jnp.take(perms, tiles % N_GRP, axis=2)
    owners = jnp.where(modes[:, :, None] == 1, paired, spread)
    return owners.reshape(N_GRP, N_CTX * TILES_DEV).astype(jnp.int32)


def touch_ends(values, own_key, smallest, largest):
    index_at = [jax.random.randint(jax.random.fold_in(own_key, axis), (), 0, length) for axis, length in enumerate(values.shape)]
    widest = values.shape.index(max(values.shape))
    next_to = index_at[:widest] + [(index_at[widest] + 1) % values.shape[widest]] + index_at[widest + 1:]
    return values.at[tuple(index_at)].set(smallest).at[tuple(next_to)].set(largest)


def steps_of(own_key, extent, shards, smallest, top_value):
    def one(dim, parts):
        draws = jax.random.uniform(jax.random.fold_in(jax.random.fold_in(own_key, 6), dim), (parts,), jnp.float32, smallest / len(shards), top_value / len(shards))
        return jnp.repeat(jnp.exp(draws), extent[dim] // parts).reshape((-1,) + (1,) * (len(extent) - dim - 1))

    loudness = one(*shards[0])
    for cut in shards[1:]:
        loudness = loudness * one(*cut)
    return loudness


def bell_draw(key, shape, width, most, cuts=(), held_as=jnp.bfloat16):
    values = width * jax.random.normal(key, shape, jnp.float32)
    if cuts:
        values = values * steps_of(key, shape, cuts, -0.22, 0.18)
    return jnp.clip(values, -most, most).astype(held_as)


def setup_inputs(seed: int = 0) -> dict:
    splits = jax.random.split(jax.random.key(seed), 15)
    clip_queries = draw_clip_queries(jax.random.fold_in(splits[14], 71), 0)
    clip_keys = draw_clip_keys(jax.random.fold_in(splits[14], 71), 0)
    clip_values = draw_clip_values(jax.random.fold_in(splits[14], 71), 0)
    cache_keys = bell_draw(splits[3], (N_GRP, CACHE, NCLIP, HEADS * HD), 1.0, 6.0, ((0, 4), (2, 32)))
    cache_values = draw_cache_values(jax.random.fold_in(splits[14], 71), 0)
    clip_pick = touch_ends(jax.random.randint(splits[5], (N_GRP, 2), 0, CACHE), jax.random.fold_in(splits[5], 1), 0, CACHE - 1).astype(jnp.int32)
    noisy_latent = bell_draw(splits[6], (N_GRP, N_CTX * TILES_DEV, LFR, TL * TL * LAT), 1.0, 6.0, ((0, 4), (1, 32)))
    prev_latent = bell_draw(splits[7], (N_GRP, N_CTX * TILES_DEV, 2, TL * TL * LAT), 1.0, 6.0, ((0, 4), (1, 32)))
    velocity_weight = bell_draw(splits[8], (HEADS * HD, 4 * LAT), (HEADS * HD) ** -0.5, 0.09375)
    tile_owner = draw_tile_owner(jax.random.fold_in(splits[14], 71), 0)
    conv_in_weight = bell_draw(splits[10], (27 * LAT, DEC_MID), (27 * LAT) ** -0.5, 0.3125)
    conv_in_bias = bell_draw(splits[11], (DEC_MID,), 1.0, 4.0, (), jnp.float32)
    conv_out_weight = bell_draw(splits[12], (9, DEC_MID, DEC_OUT), (9 * DEC_MID) ** -0.5, 0.09375)
    conv_out_bias = bell_draw(splits[13], (DEC_OUT,), 1.0, 4.0, (), jnp.float32)
    return dict(clip_queries=clip_queries, clip_keys=clip_keys, clip_values=clip_values, cache_keys=cache_keys, cache_values=cache_values, clip_pick=clip_pick, noisy_latent=noisy_latent, prev_latent=prev_latent, velocity_weight=velocity_weight, tile_owner=tile_owner, conv_in_weight=conv_in_weight, conv_in_bias=conv_in_bias, conv_out_weight=conv_out_weight, conv_out_bias=conv_out_bias)


def first_frame(rows):
    shape = rows.shape
    grouped = rows.reshape((shape[0] // (LFR * TP * TP), LFR, TP * TP) + shape[1:])
    return grouped[:, 0].reshape((-1,) + shape[1:])

def to_tiles(per_token):
    count = per_token.shape[0] // (LFR * TP * TP)
    split = per_token.reshape(count, LFR, TP, TP, 2, 2, LAT)
    return split.transpose(0, 1, 2, 4, 3, 5, 6).reshape(count, LFR, 4 * TP * TP * LAT)

def decode_tiles(stacked, conv_in_weight, conv_in_bias, conv_out_weight, conv_out_bias):
    count = stacked.shape[0]
    side = 2 * TP
    middle = conv_in_weight.shape[1]
    outer = conv_out_weight.shape[2]
    latent = stacked.reshape(count, LFR + 2, side, side, LAT)
    padded = jnp.pad(latent, ((0, 0), (0, 0), (1, 1), (1, 1), (0, 0)))
    columns = []
    for time_off in range(3):
        for row_off in range(3):
            for col_off in range(3):
                columns.append(padded[:, time_off:time_off + LFR, row_off:row_off + side, col_off:col_off + side, :])
    patches = jnp.stack(columns, axis=4).reshape(count * LFR * side * side, 27 * LAT)
    hidden = jax.nn.silu(jnp.dot(patches, conv_in_weight, preferred_element_type=jnp.float32) + conv_in_bias)
    hidden = hidden.astype(jnp.bfloat16).reshape(count, LFR, side, side, middle)
    larger = jnp.repeat(jnp.repeat(hidden, 2, axis=2), 2, axis=3)
    big_side = 2 * side
    larger = jnp.pad(larger, ((0, 0), (0, 0), (1, 1), (1, 1), (0, 0)))
    total = jnp.zeros((count * LFR * big_side * big_side, outer), jnp.float32)
    for row_off in range(3):
        for col_off in range(3):
            window = larger[:, :, row_off:row_off + big_side, col_off:col_off + big_side, :].reshape(-1, middle)
            total = total + jnp.dot(window, conv_out_weight[row_off * 3 + col_off], preferred_element_type=jnp.float32)
    return (total + conv_out_bias).astype(jnp.bfloat16).reshape(count, LFR, big_side * big_side, outer)

def tile_slots(owners, owner_count):
    count = owners.shape[0]
    slot_count = count // 2
    same = owners[:, None] == owners[None, :]
    earlier = jnp.arange(count, dtype=jnp.int32)[None, :] < jnp.arange(count, dtype=jnp.int32)[:, None]
    rank = lax.optimization_barrier(jnp.sum(jnp.where(same & earlier, 1, 0), axis=1)).astype(jnp.int32)
    target = jnp.arange(owner_count * slot_count, dtype=jnp.int32)
    return (owners[None, :] == (target // slot_count)[:, None]) & (rank[None, :] == (target % slot_count)[:, None])

def attend_video(query_rows, key_rows, value_rows):
    scale = 1.0 / math.sqrt(HD)

    def one_head(head):
        start = (head * HD).astype(jnp.int32)
        query_part = lax.dynamic_slice_in_dim(query_rows, start, HD, 1)
        key_part = lax.dynamic_slice_in_dim(key_rows, start, HD, 1)
        value_part = lax.dynamic_slice_in_dim(value_rows, start, HD, 1)
        scores = jnp.dot(query_part, key_part.T, preferred_element_type=jnp.float32) * scale
        raised = jnp.exp(scores - lax.optimization_barrier(jnp.max(scores, axis=1, keepdims=True)))
        totals = lax.optimization_barrier(jnp.sum(raised, axis=1, keepdims=True))
        mixed = jnp.dot(raised.astype(jnp.bfloat16), value_part, preferred_element_type=jnp.float32)
        return (mixed / totals).astype(jnp.bfloat16)
    per_head = lax.map(one_head, jnp.arange(HEADS, dtype=jnp.int32))
    return per_head.transpose(1, 0, 2).reshape(query_rows.shape[0], HEADS * HD)

def reference(clip_queries, clip_keys, clip_values, cache_keys, cache_values, clip_pick, noisy_latent, prev_latent, velocity_weight, tile_owner, conv_in_weight, conv_in_bias, conv_out_weight, conv_out_bias):
    outputs = []
    for video in range(N_GRP):
        sink_keys = first_frame(lax.dynamic_index_in_dim(cache_keys[video], clip_pick[video, 0], 0, keepdims=False))
        sink_values = first_frame(lax.dynamic_index_in_dim(cache_values[video], clip_pick[video, 0], 0, keepdims=False))
        window_keys = lax.dynamic_index_in_dim(cache_keys[video], clip_pick[video, 1], 0, keepdims=False)
        window_values = lax.dynamic_index_in_dim(cache_values[video], clip_pick[video, 1], 0, keepdims=False)
        all_keys = jnp.concatenate([sink_keys, window_keys, clip_keys[video]], axis=0)
        all_values = jnp.concatenate([sink_values, window_values, clip_values[video]], axis=0)
        attended = attend_video(clip_queries[video], all_keys, all_values)
        squares = lax.optimization_barrier(jnp.mean(attended.astype(jnp.float32) ** 2, axis=1, keepdims=True))
        velocity = jnp.dot(attended, velocity_weight, preferred_element_type=jnp.float32) / jnp.sqrt(squares + 1e-06)
        clean = (noisy_latent[video].astype(jnp.float32) - to_tiles(velocity)).astype(jnp.bfloat16)
        stacked = jnp.concatenate([prev_latent[video], clean], axis=1)
        outputs.append(decode_tiles(stacked, conv_in_weight, conv_in_bias, conv_out_weight, conv_out_bias))
    decoded_all = jnp.stack(outputs, axis=0)
    tail = decoded_all.shape[2:]
    decoded_all = decoded_all.reshape((N_GRP, N_CTX, TILES_DEV) + tail)
    owners = tile_owner.reshape(N_GRP, N_CTX, TILES_DEV)
    hits = jax.vmap(jax.vmap(lambda row: tile_slots(row, N_GRP)))(owners)
    hits = jnp.where(hits, 1.0, 0.0).astype(jnp.float32)
    placed = jnp.einsum('scjt,sctfpk->scjfpk', hits, decoded_all.astype(jnp.float32), precision=lax.Precision.HIGHEST)
    placed = placed.reshape((N_GRP, N_CTX, N_GRP, TILES_DEV // 2) + tail)
    return placed.transpose(2, 1, 0, 3, 4, 5, 6).astype(jnp.bfloat16)
```

```python
import functools
import math

import jax
import jax.numpy as jnp
from jax import lax
from jax.experimental import pallas as pl
from jax.experimental.pallas import tpu as pltpu
from jax.sharding import PartitionSpec as P

HEADS = 32
HD = 128
TOK = 128
F32 = jnp.float32
BF16 = jnp.bfloat16
SCALE = math.log2(math.e) / math.sqrt(HD)
HEADS_STEP = 8
BQ = 512
BK = 2048


def params(mib, axes=1):
    return pltpu.CompilerParams(
        vmem_limit_bytes=mib << 20, dimension_semantics=("arbitrary",) * axes
    )


def pack_clip_kernel(q_ref, k_ref, v_ref, out_ref):
    for head in range(HEADS_STEP):
        lanes = slice(head * HD, (head + 1) * HD)
        out_ref[head, 0:TOK, :] = q_ref[:, lanes]
        out_ref[head, TOK : 2 * TOK, :] = k_ref[:, lanes]
        out_ref[head, 2 * TOK : 3 * TOK, :] = v_ref[:, lanes]


def pack_clip(q, k, v):
    spec = pl.BlockSpec((TOK, HEADS_STEP * HD), lambda i: (0, i))
    return pl.pallas_call(
        pack_clip_kernel,
        grid=(HEADS // HEADS_STEP,),
        in_specs=[spec] * 3,
        out_specs=pl.BlockSpec((HEADS_STEP, 3 * TOK, HD), lambda i: (i, 0, 0)),
        out_shape=jax.ShapeDtypeStruct((HEADS, 3 * TOK, HD), BF16),
        compiler_params=params(24),
        name="pack_clip",
    )(q, k, v)


def pack_window_kernel(pick_ref, k_ref, v_ref, out_ref):
    for head in range(HEADS_STEP):
        lanes = slice(head * HD, (head + 1) * HD)
        out_ref[head, 0:TOK, :] = k_ref[0, :, lanes]
        out_ref[head, TOK : 2 * TOK, :] = v_ref[0, :, lanes]


def pack_sink_kernel(pick_ref, k_ref, v_ref, out_ref):
    for head in range(HEADS_STEP):
        lanes = slice(head * HD, (head + 1) * HD)
        for tile in range(4):
            rows = slice(tile * 32, tile * 32 + 16)
            out_ref[head, tile * 16 : tile * 16 + 16, :] = k_ref[0, rows, lanes]
            out_ref[head, 64 + tile * 16 : 80 + tile * 16, :] = v_ref[0, rows, lanes]


def pack_cache(pick, keys, values, which):
    body = pack_window_kernel if which == 1 else pack_sink_kernel
    rows = 2 * TOK if which == 1 else TOK
    spec = pl.BlockSpec((1, TOK, HEADS_STEP * HD), lambda i, pick: (pick[which], 0, i))
    return pl.pallas_call(
        body,
        grid_spec=pltpu.PrefetchScalarGridSpec(
            num_scalar_prefetch=1,
            grid=(HEADS // HEADS_STEP,),
            in_specs=[spec] * 2,
            out_specs=pl.BlockSpec((HEADS_STEP, rows, HD), lambda i, pick: (i, 0, 0)),
        ),
        out_shape=jax.ShapeDtypeStruct((HEADS, rows, HD), BF16),
        compiler_params=params(24),
        name="pack_window" if which == 1 else "pack_sink",
    )(pick, keys, values)


def attend_block(q, k_ref, v_ref, top, acc):
    sources, rows = k_ref.shape[0], k_ref.shape[1]
    step = min(BK // rows, sources)
    count = sources // step
    width = step * rows
    ones = jnp.ones((width, HD), BF16)

    def score(j):
        k = k_ref[j * step : (j + 1) * step].reshape(width, HD)
        return lax.dot_general(q, k, (((1,), (1,)), ((), ())), preferred_element_type=F32)

    following = score(0)
    for j in range(count):
        scores = following
        if j + 1 < count:
            following = score(j + 1)
        high = jnp.max(scores, axis=1, keepdims=True)
        if top is not None:
            high = jnp.maximum(top, high)
        raised = jnp.exp2((scores - high) * SCALE).astype(BF16)
        v = v_ref[j * step : (j + 1) * step].reshape(width, HD)
        mixed = jnp.dot(raised, jnp.concatenate([v, ones], axis=1), preferred_element_type=F32)
        if top is None:
            acc = mixed
        else:
            acc = acc * jnp.exp2((top - high) * SCALE) + mixed
        top = high
    return top, acc


def attend_first_kernel(q_ref, k_ref, v_ref, top_ref, acc_ref):
    q = q_ref[...].reshape(BQ, HD)
    top, acc = attend_block(q, k_ref, v_ref, None, None)
    top_ref[...] = jnp.broadcast_to(top, (BQ, HD))
    acc_ref[...] = acc


def attend_next_kernel(q_ref, k_ref, v_ref, top_in_ref, acc_in_ref, top_ref, acc_ref):
    q = q_ref[...].reshape(BQ, HD)
    top, acc = attend_block(q, k_ref, v_ref, top_in_ref[:, :1], acc_in_ref[...])
    top_ref[...] = jnp.broadcast_to(top, (BQ, HD))
    acc_ref[...] = acc


def attend_last_kernel(
    q_ref, k_ref, v_ref, top_in_ref, acc_in_ref, weight_ref, gather_ref, out_ref, rows_ref
):
    q = q_ref[...].reshape(BQ, HD)
    _, acc = attend_block(q, k_ref, v_ref, top_in_ref[:, :1], acc_in_ref[...])
    rows_ref[...] = acc[:, :HD] / acc[:, HD:]
    parts = [rows_ref[pl.ds(px, BQ // 4, stride=4), :].astype(BF16) for px in range(4)]
    attended = jnp.concatenate(parts, axis=1)
    moved = jnp.dot(attended, weight_ref[...], preferred_element_type=F32).astype(BF16)
    wide = attended.astype(F32)
    squares = jnp.dot((wide * wide).astype(BF16), gather_ref[...], preferred_element_type=F32)
    dests = BQ // TOK
    out_ref[:, 0:32, :] = moved[:, :HD].reshape(dests, 32, HD)
    out_ref[:, 32:64, :] = moved[:, HD:].reshape(dests, 32, HD)
    out_ref[:, 64:96, :] = squares.astype(BF16).reshape(dests, 32, HD)


def attend(kind, first, keys_values, k_rows, k_place, state=(), extra=()):
    sources = HEADS
    total = sources * TOK
    blocks = BQ // TOK
    q_spec = pl.BlockSpec((blocks, TOK, HD), lambda i: (i, 0, 0))
    k_spec = pl.BlockSpec((sources, k_rows, HD), lambda i: (0, k_place, 0))
    v_spec = pl.BlockSpec((sources, k_rows, HD), lambda i: (0, k_place + 1, 0))
    state_specs = [
        pl.BlockSpec((BQ, HD), lambda i: (i, 0)),
        pl.BlockSpec((BQ, 2 * HD), lambda i: (i, 0)),
    ]
    state_shapes = [
        jax.ShapeDtypeStruct((total, HD), F32),
        jax.ShapeDtypeStruct((total, 2 * HD), F32),
    ]
    in_specs = [q_spec, k_spec, v_spec] + (state_specs if state else [])
    scratch = []
    if kind == "last":
        body = attend_last_kernel
        in_specs += [pl.BlockSpec(x.shape, lambda i: (0, 0)) for x in extra]
        out_specs = pl.BlockSpec((blocks, 96, HD), lambda i: (i, 0, 0))
        out_shape = jax.ShapeDtypeStruct((sources, 96, HD), BF16)
        scratch = [pltpu.VMEM((BQ, HD), F32)]
    else:
        body = attend_next_kernel if state else attend_first_kernel
        out_specs, out_shape = state_specs, state_shapes
    keys = sources * k_rows
    return pl.pallas_call(
        body,
        grid=(total // BQ,),
        in_specs=in_specs,
        out_specs=out_specs,
        out_shape=out_shape,
        scratch_shapes=scratch,
        compiler_params=params(48),
        cost_estimate=pl.CostEstimate(
            flops=8 * total * keys * HD,
            transcendentals=total * keys,
            bytes_accessed=8 << 20,
        ),
        name="attend_" + kind,
    )(first, keys_values, keys_values, *state, *extra)


def clean_kernel(owner_ref, parts_ref, noisy_ref, prev_ref, out_ref):
    width = HEADS * HD
    sums = jnp.sum(parts_ref[...].astype(F32), axis=0)
    scale = 1.0 / jnp.sqrt(sums[64:96] * (1.0 / width) + 1e-06)
    noisy = noisy_ref[...].astype(F32)
    prev = prev_ref[...].astype(F32)
    clean = [noisy[i * 32 : i * 32 + 32] - sums[i * 32 : i * 32 + 32] * scale for i in range(2)]
    owners = [owner_ref[t] for t in range(4)]
    ranks = []
    for t in range(4):
        rank = jnp.int32(0)
        for earlier in range(t):
            rank = rank + jnp.where(owners[earlier] == owners[t], 1, 0)
        ranks.append(rank)
    zero = jnp.zeros((8, HD), F32)
    for owner in range(4):
        rows = []
        for slot in range(2):
            picked = [zero] * 5
            for t in range(4):
                here = (owners[t] == owner) & (ranks[t] == slot)
                piece = slice(t * 8, t * 8 + 8)
                pieces = (
                    prev[0:32][piece],
                    prev[32:64][piece],
                    clean[0][piece],
                    clean[1][piece],
                    jnp.ones((8, HD), F32),
                )
                picked = [jnp.where(here, new, old) for new, old in zip(pieces, picked)]
            rows += picked
        out_ref[owner] = jnp.concatenate(rows, axis=0).astype(BF16)


def clean_and_place(owner, parts, noisy, prev):
    vmem = pl.BlockSpec(memory_space=pltpu.VMEM)
    return pl.pallas_call(
        clean_kernel,
        in_specs=[pl.BlockSpec(memory_space=pltpu.SMEM), vmem, vmem, vmem],
        out_specs=vmem,
        out_shape=jax.ShapeDtypeStruct((4, 80, HD), BF16),
        compiler_params=pltpu.CompilerParams(vmem_limit_bytes=16 << 20),
        name="clean_and_place",
    )(owner, parts, noisy, prev)


def shift_rows(x, by):
    moved = pltpu.roll(x, by % 8, axis=1)
    y = lax.broadcasted_iota(jnp.int32, x.shape, 1)
    return jnp.where((y >= by) if by > 0 else (y < 8 + by), moved, 0.0)


def decode_kernel(
    in_ref, w_in_ref, b_in_ref, w_out_ref, b_out_ref, out_ref, latent_ref, part_ref, wide_ref
):
    tiles = 8
    flags = []
    for tile in range(tiles):
        block = in_ref[tile // 2, (tile % 2) * 40 : (tile % 2) * 40 + 40, :].astype(F32)
        for frames in range(2):
            for i in range(2):
                at = frames * 16 + i * 8
                latent_ref[pl.ds(tile * 32 + frames * 16 + i, 8, stride=2), :] = block[at : at + 8]
        flags.append(block[32:33])
    latent = latent_ref[...].reshape(tiles * 4, 8, HD)
    by_row = [shift_rows(latent, 1), latent, shift_rows(latent, -1)]
    by_row = [x.reshape(tiles * 32, HD) for x in by_row]
    lane = lax.broadcasted_iota(jnp.int32, (tiles * 32, HD), 1)
    low = lane < 64
    hidden = []
    for x in range(8):
        turn = (16 - 16 * x) % HD
        pair = [
            pltpu.roll(by_row[0], turn, axis=1) if turn else by_row[0],
            pltpu.roll(by_row[1], (turn + 64) % HD, axis=1) if turn != 64 else by_row[1],
            pltpu.roll(by_row[2], turn, axis=1) if turn else by_row[2],
        ]
        left = jnp.where(low, pair[0], pair[1])
        right = jnp.where(low, pair[2], 0.0)
        if x == 0:
            keep = (lane & 63) >= 16
            left, right = jnp.where(keep, left, 0.0), jnp.where(keep, right, 0.0)
        if x == 7:
            keep = (lane & 63) < 32
            left, right = jnp.where(keep, left, 0.0), jnp.where(keep, right, 0.0)
        taps = jnp.concatenate([left, right], axis=1).reshape(tiles, 4, 8, 2 * HD)
        columns = jnp.concatenate(
            [taps[:, dt : dt + 2].reshape(TOK, 2 * HD).astype(BF16) for dt in range(3)], axis=1
        )
        mid = jnp.dot(columns, w_in_ref[...], preferred_element_type=F32) + b_in_ref[...]
        hidden.append(mid / (1.0 + jnp.exp(-mid)))
    bias = b_out_ref[...]
    for a in range(2):
        for x in range(8):
            here = hidden[x]
            grouped = here.reshape(16, 8, 512)
            other = shift_rows(grouped, 1 if a == 0 else -1).reshape(TOK, 512)
            pair = [other, here] if a == 0 else [here, other]
            rows = jnp.concatenate([p.astype(BF16) for p in pair], axis=1)
            part_ref[x * TOK : (x + 1) * TOK, :] = jnp.dot(
                rows, w_out_ref[a], preferred_element_type=F32
            )
        for x in range(8):
            at = x * TOK
            first = part_ref[at : at + TOK, 128:256] + bias
            if x > 0:
                first = first + part_ref[at - TOK : at, 0:128]
            second = part_ref[at : at + TOK, 256:384] + bias
            if x < 7:
                second = second + part_ref[at + TOK : at + 2 * TOK, 384:512]
            wide_ref[pl.ds(a * 16 + 2 * x, TOK, stride=32), :] = first
            wide_ref[pl.ds(a * 16 + 2 * x + 1, TOK, stride=32), :] = second
    for tile in range(tiles):
        rows = slice(tile * 512, tile * 512 + 512)
        out_ref[rows, :] = jnp.where(flags[tile] > 0.5, wide_ref[rows, :], 0.0).astype(BF16)


def decode(arrived, w_in, b_in, w_out, b_out):
    vmem = pl.BlockSpec(memory_space=pltpu.VMEM)
    return pl.pallas_call(
        decode_kernel,
        in_specs=[vmem] * 5,
        out_specs=vmem,
        out_shape=jax.ShapeDtypeStruct((8 * 512, HD), BF16),
        scratch_shapes=[
            pltpu.VMEM((256, HD), F32),
            pltpu.VMEM((8 * TOK, 512), F32),
            pltpu.VMEM((8 * 512, HD), F32),
        ],
        compiler_params=pltpu.CompilerParams(vmem_limit_bytes=48 << 20),
        name="decode",
    )(arrived, w_in, b_in, w_out, b_out)


def place_velocity_weight(velocity_weight):
    head = lax.axis_index("ctx")
    mine = lax.dynamic_slice_in_dim(velocity_weight, head * HD, HD, 0).reshape(HD, 2, 32)
    same = jnp.eye(4, dtype=BF16)
    placed = mine[None, :, :, None, :] * same[:, None, None, :, None]
    gather = jnp.broadcast_to(same[:, None, :, None], (4, HD, 4, 32))
    return placed.reshape(4 * HD, 2 * HD), gather.reshape(4 * HD, HD)


def place_in_weight(weight):
    split = weight.reshape(3, 3, 48, 512)
    return jnp.pad(split, ((0, 0), (0, 1), (0, 16), (0, 0))).reshape(3 * 4 * 64, 512)


def place_out_weight(weight):
    w = weight.reshape(3, 3, 512, 128).astype(F32)
    rows = [[w[0], w[1] + w[2]], [w[0] + w[1], w[2]]]
    phases = []
    for a in range(2):
        halves = []
        for r in rows[a]:
            halves.append(jnp.concatenate([r[0], r[1] + r[2], r[0] + r[1], r[2]], axis=1))
        phases.append(jnp.concatenate(halves, axis=0))
    return jnp.stack(phases).astype(BF16)


def latent_rows(latent):
    return latent.reshape(4, 2, 4, 2, HD).transpose(3, 0, 1, 2, 4).reshape(64, HD)


def exchange(x, axis):
    return lax.all_to_all(x, axis, split_axis=0, concat_axis=0, tiled=True)


def local(
    clip_queries,
    clip_keys,
    clip_values,
    cache_keys,
    cache_values,
    clip_pick,
    noisy_latent,
    prev_latent,
    velocity_weight,
    tile_owner,
    conv_in_weight,
    conv_in_bias,
    conv_out_weight,
    conv_out_bias,
):
    pick = clip_pick[0]
    clip = exchange(pack_clip(clip_queries[0], clip_keys[0], clip_values[0]), "ctx")
    window = pack_cache(pick, cache_keys[0], cache_values[0], 1)
    sink = pack_cache(pick, cache_keys[0], cache_values[0], 0)
    weight, gather = place_velocity_weight(velocity_weight)
    w_in = place_in_weight(conv_in_weight)
    w_out = place_out_weight(conv_out_weight)
    noisy = latent_rows(noisy_latent[0])
    prev = latent_rows(prev_latent[0])

    clip, window, sink, weight, gather, w_in, w_out, noisy, prev = lax.optimization_barrier(
        (clip, window, sink, weight, gather, w_in, w_out, noisy, prev)
    )
    window = exchange(window, "ctx")
    state = attend("first", clip, clip, TOK, 1)
    window, sink = lax.optimization_barrier((window, sink))
    sink = exchange(sink, "ctx")
    state = attend("next", clip, window, TOK, 0, state)
    parts = attend("last", clip, sink, TOK // 2, 0, state, (weight, gather))
    parts = exchange(parts, "ctx")
    outgoing = clean_and_place(tile_owner[0], parts, noisy, prev)
    arrived = exchange(outgoing, "grp")
    decoded = decode(
        arrived, w_in, conv_in_bias.reshape(1, -1), w_out, conv_out_bias.reshape(1, -1)
    )
    return decoded.reshape(1, 1, 4, 2, 2, 256, 128)


def solution(mesh):
    in_specs = (
        P("grp", "ctx", None),
        P("grp", "ctx", None),
        P("grp", "ctx", None),
        P("grp", None, "ctx", None),
        P("grp", None, "ctx", None),
        P("grp", None),
        P("grp", "ctx", None, None),
        P("grp", "ctx", None, None),
        P(),
        P("grp", "ctx"),
        P(),
        P(),
        P(),
        P(),
    )
    out_specs = P("grp", "ctx", None, None, None, None, None)
    return jax.shard_map(local, mesh=mesh, in_specs=in_specs, out_specs=out_specs, check_vma=False)
```

```python
import math

import jax
import jax.numpy as jnp
from jax import lax
from jax.experimental import pallas as pl
from jax.experimental.pallas import tpu as pltpu
from jax.sharding import PartitionSpec as P

HEADS = 32
HD = 128
TOK = 128
F32 = jnp.float32
BF16 = jnp.bfloat16
SCALE = math.log2(math.e) / math.sqrt(HD)
HEADS_STEP = 8
BQ = 1024
LIMIT = 110.0


def params(mib, axes=1):
    return pltpu.CompilerParams(
        vmem_limit_bytes=mib << 20, dimension_semantics=("arbitrary",) * axes
    )


def pack_first_kernel(pick_ref, q_ref, k_ref, v_ref, sink_k_ref, sink_v_ref, out_ref):
    for head in range(HEADS_STEP):
        lanes = slice(head * HD, (head + 1) * HD)
        out_ref[head, 0:TOK, :] = k_ref[:, lanes]
        out_ref[head, 192 : 192 + TOK, :] = v_ref[:, lanes]
        out_ref[head, 384 : 384 + TOK, :] = q_ref[:, lanes]
        for tile in range(4):
            rows = slice(tile * 32, tile * 32 + 16)
            at = TOK + tile * 16
            out_ref[head, at : at + 16, :] = sink_k_ref[0, rows, lanes]
            out_ref[head, 192 + at : 208 + at, :] = sink_v_ref[0, rows, lanes]


def pack_window_kernel(pick_ref, k_ref, v_ref, out_ref):
    for head in range(HEADS_STEP):
        lanes = slice(head * HD, (head + 1) * HD)
        out_ref[head, 0:TOK, :] = k_ref[0, :, lanes]
        out_ref[head, TOK : 2 * TOK, :] = v_ref[0, :, lanes]


def pack(pick, current, keys, values, which):
    rows = 2 * TOK if which == 1 else 4 * TOK
    own = pl.BlockSpec((TOK, HEADS_STEP * HD), lambda i, pick: (0, i))
    cached = pl.BlockSpec((1, TOK, HEADS_STEP * HD), lambda i, pick: (pick[which], 0, i))
    return pl.pallas_call(
        pack_window_kernel if which == 1 else pack_first_kernel,
        grid_spec=pltpu.PrefetchScalarGridSpec(
            num_scalar_prefetch=1,
            grid=(HEADS // HEADS_STEP,),
            in_specs=[own] * len(current) + [cached] * 2,
            out_specs=pl.BlockSpec((HEADS_STEP, rows, HD), lambda i, pick: (i, 0, 0)),
        ),
        out_shape=jax.ShapeDtypeStruct((HEADS, rows, HD), BF16),
        compiler_params=params(60),
        name="pack_window" if which == 1 else "pack_first",
    )(pick, *current, keys, values)


def key_blocks(ref, step):
    sources, rows = ref.shape[0], ref.shape[1]
    return [
        ref[j : j + step].reshape(step * rows, HD) for j in range(0, sources, step)
    ]


def score(k, q):
    return lax.dot_general(k, q, (((1,), (1,)), ((), ())), preferred_element_type=F32)


def mix(v, raised):
    return lax.dot_general(
        v, raised.astype(BF16), (((0,), (0,)), ((), ())), preferred_element_type=F32
    )


def fold_rows(x):
    return jnp.sum(x.reshape(x.shape[0] // 8, 8, x.shape[1]), axis=0)


def attend_bounded(q, k_ref, v_ref, step, totals_ref, acc_ref, add):
    keys, values = key_blocks(k_ref, step), key_blocks(v_ref, step)
    totals = totals_ref[...] if add else None
    acc = acc_ref[...] if add else None
    following = score(keys[0], q)
    for j in range(len(keys)):
        scores = following
        if j + 1 < len(keys):
            following = score(keys[j + 1], q)
        raised = jnp.exp2(scores * SCALE)
        mixed, total = mix(values[j], raised), fold_rows(raised)
        acc = mixed if acc is None else acc + mixed
        totals = total if totals is None else totals + total
    totals_ref[...] = totals
    acc_ref[...] = acc


def attend_any(q, k_ref, v_ref, step, top_ref, totals_ref, acc_ref, add):
    sources, rows = k_ref.shape[0], k_ref.shape[1]
    if not add:
        top_ref[...] = jnp.full(top_ref.shape, -1e30, F32)
        totals_ref[...] = jnp.zeros(totals_ref.shape, F32)
        acc_ref[...] = jnp.zeros(acc_ref.shape, F32)

    def body(j, carry):
        here = pl.ds(j * step, step)
        scores = score(k_ref[here].reshape(step * rows, HD), q)
        before = top_ref[0:1, :]
        top = jnp.maximum(before, jnp.max(scores, axis=0, keepdims=True))
        raised = jnp.exp2((scores - top) * SCALE)
        fade = jnp.exp2((before - top) * SCALE)
        mixed = mix(v_ref[here].reshape(step * rows, HD), raised)
        acc_ref[...] = acc_ref[...] * fade + mixed
        totals_ref[...] = totals_ref[...] * fade + fold_rows(raised)
        top_ref[...] = jnp.broadcast_to(top, top_ref.shape)
        return carry

    lax.fori_loop(0, sources // step, body, 0)


def bounded(q, k_ref, widest_ref):
    @pl.when(pl.program_id(0) == 0)
    def _():
        widest = jnp.max(jnp.abs(k_ref[...].reshape(-1, HD)), axis=0, keepdims=True)
        widest_ref[...] = jnp.broadcast_to(widest.astype(F32), widest_ref.shape)

    widest = widest_ref[...].astype(BF16)
    reach = lax.dot_general(
        widest, jnp.abs(q), (((1,), (1,)), ((), ())), preferred_element_type=F32
    )
    return jnp.max(reach[0:8]) * (1.01 * SCALE) <= LIMIT


def attend_first_kernel(q_ref, k_ref, v_ref, slow_ref, top_ref, totals_ref, acc_ref, widest_ref):
    q = q_ref[...].reshape(BQ, HD)
    fits = bounded(q, k_ref, widest_ref)
    slow_ref[pl.program_id(0)] = jnp.where(fits, 0, 1)

    @pl.when(fits)
    def _():
        top_ref[...] = jnp.zeros(top_ref.shape, F32)
        attend_bounded(q, k_ref, v_ref, 4, totals_ref, acc_ref, False)

    @pl.when(jnp.logical_not(fits))
    def _():
        attend_any(q, k_ref, v_ref, 4, top_ref, totals_ref, acc_ref, False)


def attend_last_kernel(
    q_ref, k_ref, v_ref, slow_ref, top_in_ref, totals_in_ref, acc_in_ref, weight_ref,
    out_ref, top_ref, totals_ref, acc_ref, widest_ref,
):
    q = q_ref[...].reshape(BQ, HD)
    fits = bounded(q, k_ref, widest_ref) & (slow_ref[pl.program_id(0)] == 0)
    totals_ref[...] = totals_in_ref[...]
    acc_ref[...] = acc_in_ref[...]

    @pl.when(fits)
    def _():
        attend_bounded(q, k_ref, v_ref, 8, totals_ref, acc_ref, True)

    @pl.when(jnp.logical_not(fits))
    def _():
        top_ref[...] = top_in_ref[...]
        attend_any(q, k_ref, v_ref, 8, top_ref, totals_ref, acc_ref, True)

    totals = jnp.sum(totals_ref[...], axis=0, keepdims=True)
    attended = (acc_ref[...] / totals).astype(BF16)
    moved = lax.dot_general(
        weight_ref[...], attended, (((0,), (0,)), ((), ())), preferred_element_type=F32
    )
    wide = attended.astype(F32)
    squares = jnp.broadcast_to(jnp.sum(wide * wide, axis=0, keepdims=True), (8, BQ))
    block = jnp.concatenate([moved, squares], axis=0).astype(BF16)
    for dest in range(BQ // TOK):
        out_ref[dest] = block[:, dest * TOK : (dest + 1) * TOK]


def attend(kind, queries, keys_values, k_rows, state=(), weight=None):
    total = HEADS * TOK
    blocks = BQ // TOK
    steps = total // BQ
    q_spec = pl.BlockSpec((blocks, TOK, HD), lambda i: (i, 3, 0))
    k_spec = pl.BlockSpec((HEADS, k_rows, HD), lambda i: (0, 0, 0))
    v_spec = pl.BlockSpec((HEADS, k_rows, HD), lambda i: (0, 1, 0))
    state_specs = [
        pl.BlockSpec(memory_space=pltpu.SMEM),
        pl.BlockSpec((8, BQ), lambda i: (0, i)),
        pl.BlockSpec((8, BQ), lambda i: (0, i)),
        pl.BlockSpec((HD, BQ), lambda i: (0, i)),
    ]
    state_shapes = [
        jax.ShapeDtypeStruct((steps,), jnp.int32),
        jax.ShapeDtypeStruct((8, total), F32),
        jax.ShapeDtypeStruct((8, total), F32),
        jax.ShapeDtypeStruct((HD, total), F32),
    ]
    in_specs = [q_spec, k_spec, v_spec]
    scratch = [pltpu.VMEM((16, HD), F32)]
    args = (queries, keys_values, keys_values)
    if kind == "first":
        body, out_specs, out_shape = attend_first_kernel, state_specs, state_shapes
    else:
        body = attend_last_kernel
        in_specs += state_specs + [pl.BlockSpec(weight.shape, lambda i: (0, 0))]
        args += (*state, weight)
        out_specs = pl.BlockSpec((blocks, 72, HD), lambda i: (i, 0, 0))
        out_shape = jax.ShapeDtypeStruct((HEADS, 72, HD), BF16)
        scratch = [
            pltpu.VMEM((8, BQ), F32),
            pltpu.VMEM((8, BQ), F32),
            pltpu.VMEM((HD, BQ), F32),
        ] + scratch
    keys = HEADS * k_rows
    return pl.pallas_call(
        body,
        grid=(steps,),
        in_specs=in_specs,
        out_specs=out_specs,
        out_shape=out_shape,
        scratch_shapes=scratch,
        compiler_params=params(48),
        cost_estimate=pl.CostEstimate(
            flops=6 * total * keys * HD,
            transcendentals=total * keys,
            bytes_accessed=8 << 20,
        ),
        name="attend_" + kind,
    )(*args)


def clean_kernel(owner_ref, parts_ref, noisy_ref, prev_ref, out_ref, token_ref):
    width = HEADS * HD
    sums = jnp.sum(parts_ref[...].astype(F32), axis=0)
    scale = 1.0 / jnp.sqrt(sums[64:65] * (1.0 / width) + 1e-06)
    velocity = sums[0:64] * scale
    velocity = jnp.concatenate([velocity, jnp.zeros((64, HD), F32)], axis=0)
    token_ref[...] = jnp.transpose(velocity)
    lane = lax.broadcasted_iota(jnp.int32, (32, HD), 1)
    clean = []
    by_px = [token_ref[pl.ds(px, 32, stride=4), :] for px in range(4)]
    for i in range(2):
        moved = jnp.zeros((32, HD), F32)
        for px in range(4):
            turn = (px - i) * 32 % HD
            piece = pltpu.roll(by_px[px], turn, axis=1) if turn else by_px[px]
            moved = jnp.where(lane // 32 == px, piece, moved)
        clean.append(noisy_ref[i * 32 : i * 32 + 32, :].astype(F32) - moved)
    prev = prev_ref[...].astype(F32)
    owners = [owner_ref[t] for t in range(4)]
    ranks = []
    for t in range(4):
        rank = jnp.int32(0)
        for earlier in range(t):
            rank = rank + jnp.where(owners[earlier] == owners[t], 1, 0)
        ranks.append(rank)
    zero = jnp.zeros((8, HD), F32)
    for owner in range(4):
        rows = []
        for slot in range(2):
            picked = [zero] * 5
            for t in range(4):
                here = (owners[t] == owner) & (ranks[t] == slot)
                piece = slice(t * 8, t * 8 + 8)
                pieces = (
                    prev[0:32][piece],
                    prev[32:64][piece],
                    clean[0][piece],
                    clean[1][piece],
                    jnp.ones((8, HD), F32),
                )
                picked = [jnp.where(here, new, old) for new, old in zip(pieces, picked)]
            rows += picked
        out_ref[owner] = jnp.concatenate(rows, axis=0).astype(BF16)


def clean_and_place(owner, parts, noisy, prev):
    vmem = pl.BlockSpec(memory_space=pltpu.VMEM)
    return pl.pallas_call(
        clean_kernel,
        in_specs=[pl.BlockSpec(memory_space=pltpu.SMEM), vmem, vmem, vmem],
        out_specs=vmem,
        out_shape=jax.ShapeDtypeStruct((4, 80, HD), BF16),
        scratch_shapes=[pltpu.VMEM((HD, HD), F32)],
        compiler_params=pltpu.CompilerParams(vmem_limit_bytes=16 << 20),
        name="clean_and_place",
    )(owner, parts, noisy, prev)


def shift_rows(x, by):
    moved = pltpu.roll(x, by % 8, axis=1)
    y = lax.broadcasted_iota(jnp.int32, x.shape, 1)
    return jnp.where((y >= by) if by > 0 else (y < 8 + by), moved, 0.0)


def decode_kernel(
    in_ref, w_in_ref, b_in_ref, w_out_ref, b_out_ref, out_ref, latent_ref, part_ref, wide_ref
):
    tiles = 8
    flags = []
    for tile in range(tiles):
        block = in_ref[tile // 2, (tile % 2) * 40 : (tile % 2) * 40 + 40, :].astype(F32)
        for frames in range(2):
            for i in range(2):
                at = frames * 16 + i * 8
                latent_ref[pl.ds(tile * 32 + frames * 16 + i, 8, stride=2), :] = block[at : at + 8]
        flags.append(block[32:33])
    latent = latent_ref[...].reshape(tiles * 4, 8, HD)
    by_row = [shift_rows(latent, 1), latent, shift_rows(latent, -1)]
    by_row = [x.reshape(tiles * 32, HD) for x in by_row]
    lane = lax.broadcasted_iota(jnp.int32, (tiles * 32, HD), 1)
    low = lane < 64
    hidden = []
    for x in range(8):
        turn = (16 - 16 * x) % HD
        pair = [
            pltpu.roll(by_row[0], turn, axis=1) if turn else by_row[0],
            pltpu.roll(by_row[1], (turn + 64) % HD, axis=1) if turn != 64 else by_row[1],
            pltpu.roll(by_row[2], turn, axis=1) if turn else by_row[2],
        ]
        left = jnp.where(low, pair[0], pair[1])
        right = jnp.where(low, pair[2], 0.0)
        if x == 0:
            keep = (lane & 63) >= 16
            left, right = jnp.where(keep, left, 0.0), jnp.where(keep, right, 0.0)
        if x == 7:
            keep = (lane & 63) < 32
            left, right = jnp.where(keep, left, 0.0), jnp.where(keep, right, 0.0)
        taps = jnp.concatenate([left, right], axis=1).reshape(tiles, 4, 8, 2 * HD)
        columns = jnp.concatenate(
            [taps[:, dt : dt + 2].reshape(TOK, 2 * HD).astype(BF16) for dt in range(3)], axis=1
        )
        mid = jnp.dot(columns, w_in_ref[...], preferred_element_type=F32) + b_in_ref[...]
        hidden.append(mid / (1.0 + jnp.exp(-mid)))
    bias = b_out_ref[...]
    for a in range(2):
        for x in range(8):
            here = hidden[x]
            grouped = here.reshape(16, 8, 512)
            other = shift_rows(grouped, 1 if a == 0 else -1).reshape(TOK, 512)
            pair = [other, here] if a == 0 else [here, other]
            rows = jnp.concatenate([p.astype(BF16) for p in pair], axis=1)
            part_ref[x * TOK : (x + 1) * TOK, :] = jnp.dot(
                rows, w_out_ref[a], preferred_element_type=F32
            )
        for x in range(8):
            at = x * TOK
            first = part_ref[at : at + TOK, 128:256] + bias
            if x > 0:
                first = first + part_ref[at - TOK : at, 0:128]
            second = part_ref[at : at + TOK, 256:384] + bias
            if x < 7:
                second = second + part_ref[at + TOK : at + 2 * TOK, 384:512]
            wide_ref[pl.ds(a * 16 + 2 * x, TOK, stride=32), :] = first
            wide_ref[pl.ds(a * 16 + 2 * x + 1, TOK, stride=32), :] = second
    for tile in range(tiles):
        rows = slice(tile * 512, tile * 512 + 512)
        out_ref[rows, :] = jnp.where(flags[tile] > 0.5, wide_ref[rows, :], 0.0).astype(BF16)


def decode(arrived, w_in, b_in, w_out, b_out):
    vmem = pl.BlockSpec(memory_space=pltpu.VMEM)
    return pl.pallas_call(
        decode_kernel,
        in_specs=[vmem] * 5,
        out_specs=vmem,
        out_shape=jax.ShapeDtypeStruct((8 * 512, HD), BF16),
        scratch_shapes=[
            pltpu.VMEM((256, HD), F32),
            pltpu.VMEM((8 * TOK, 512), F32),
            pltpu.VMEM((8 * 512, HD), F32),
        ],
        compiler_params=pltpu.CompilerParams(vmem_limit_bytes=48 << 20),
        name="decode",
    )(arrived, w_in, b_in, w_out, b_out)


def head_weight(velocity_weight):
    head = lax.axis_index("ctx")
    return lax.dynamic_slice_in_dim(velocity_weight, head * HD, HD, 0)


def place_in_weight(weight):
    split = weight.reshape(3, 3, 48, 512)
    return jnp.pad(split, ((0, 0), (0, 1), (0, 16), (0, 0))).reshape(3 * 4 * 64, 512)


def place_out_weight(weight):
    w = weight.reshape(3, 3, 512, 128).astype(F32)
    rows = [[w[0], w[1] + w[2]], [w[0] + w[1], w[2]]]
    phases = []
    for a in range(2):
        halves = []
        for r in rows[a]:
            halves.append(jnp.concatenate([r[0], r[1] + r[2], r[0] + r[1], r[2]], axis=1))
        phases.append(jnp.concatenate(halves, axis=0))
    return jnp.stack(phases).astype(BF16)


def latent_rows(latent):
    return latent.reshape(4, 2, 4, 2, HD).transpose(3, 0, 1, 2, 4).reshape(64, HD)


def exchange(x, axis):
    return lax.all_to_all(x, axis, split_axis=0, concat_axis=0, tiled=True)


def local(
    clip_queries,
    clip_keys,
    clip_values,
    cache_keys,
    cache_values,
    clip_pick,
    noisy_latent,
    prev_latent,
    velocity_weight,
    tile_owner,
    conv_in_weight,
    conv_in_bias,
    conv_out_weight,
    conv_out_bias,
):
    pick = clip_pick[0]
    current = (clip_queries[0], clip_keys[0], clip_values[0])
    clip = exchange(pack(pick, current, cache_keys[0], cache_values[0], 0), "ctx")
    window = pack(pick, (), cache_keys[0], cache_values[0], 1)
    weight = head_weight(velocity_weight)
    w_in = place_in_weight(conv_in_weight)
    w_out = place_out_weight(conv_out_weight)
    noisy = latent_rows(noisy_latent[0])
    prev = latent_rows(prev_latent[0])

    clip, window, weight, w_in, w_out, noisy, prev = lax.optimization_barrier(
        (clip, window, weight, w_in, w_out, noisy, prev)
    )
    window = exchange(window, "ctx")
    state = attend("first", clip, clip, 192)
    parts = attend("last", clip, window, TOK, state, weight)
    parts = exchange(parts, "ctx")
    outgoing = clean_and_place(tile_owner[0], parts, noisy, prev)
    arrived = exchange(outgoing, "grp")
    decoded = decode(
        arrived, w_in, conv_in_bias.reshape(1, -1), w_out, conv_out_bias.reshape(1, -1)
    )
    return decoded.reshape(1, 1, 4, 2, 2, 256, 128)


def solution(mesh):
    in_specs = (
        P("grp", "ctx", None),
        P("grp", "ctx", None),
        P("grp", "ctx", None),
        P("grp", None, "ctx", None),
        P("grp", None, "ctx", None),
        P("grp", None),
        P("grp", "ctx", None, None),
        P("grp", "ctx", None, None),
        P(),
        P("grp", "ctx"),
        P(),
        P(),
        P(),
        P(),
    )
    out_specs = P("grp", "ctx", None, None, None, None, None)
    return jax.shard_map(local, mesh=mesh, in_specs=in_specs, out_specs=out_specs, check_vma=False)
```

```python
import math

import jax
import jax.numpy as jnp
from jax import lax
from jax.experimental import pallas as pl
from jax.experimental.pallas import tpu as pltpu
from jax.sharding import PartitionSpec as P

HEADS = 32
HD = 128
TOK = 128
F32 = jnp.float32
BF16 = jnp.bfloat16
SCALE = math.log2(math.e) / math.sqrt(HD)
HEADS_STEP = 8
BQ = 2048
LIMIT = 110.0


def params(mib, axes=1):
    return pltpu.CompilerParams(
        vmem_limit_bytes=mib << 20, dimension_semantics=("arbitrary",) * axes
    )


def pack_first_kernel(pick_ref, q_ref, k_ref, v_ref, sink_k_ref, sink_v_ref, out_ref):
    for head in range(out_ref.shape[0]):
        lanes = slice(head * HD, (head + 1) * HD)
        out_ref[head, 0:TOK, :] = k_ref[:, lanes]
        out_ref[head, 192 : 192 + TOK, :] = v_ref[:, lanes]
        out_ref[head, 384 : 384 + TOK, :] = q_ref[:, lanes]
        for tile in range(4):
            rows = slice(tile * 32, tile * 32 + 16)
            at = TOK + tile * 16
            out_ref[head, at : at + 16, :] = sink_k_ref[0, rows, lanes]
            out_ref[head, 192 + at : 208 + at, :] = sink_v_ref[0, rows, lanes]


def pack_first(pick, current, keys, values):
    heads = 2 * HEADS_STEP
    own = pl.BlockSpec((TOK, heads * HD), lambda i, pick: (0, i))
    cached = pl.BlockSpec((1, TOK, heads * HD), lambda i, pick: (pick[0], 0, i))
    return pl.pallas_call(
        pack_first_kernel,
        grid_spec=pltpu.PrefetchScalarGridSpec(
            num_scalar_prefetch=1,
            grid=(HEADS // heads,),
            in_specs=[own] * 3 + [cached] * 2,
            out_specs=pl.BlockSpec((heads, 4 * TOK, HD), lambda i, pick: (i, 0, 0)),
        ),
        out_shape=jax.ShapeDtypeStruct((HEADS, 4 * TOK, HD), BF16),
        compiler_params=params(60),
        name="pack_first",
    )(pick, *current, keys, values)


def pack_window_kernel(pick_ref, k_ref, v_ref, out_ref):
    for head in range(HEADS_STEP):
        lanes = slice(head * HD, (head + 1) * HD)
        out_ref[head, 0:TOK, :] = k_ref[0, :, lanes]
        out_ref[head, TOK : 2 * TOK, :] = v_ref[0, :, lanes]


def pack_window(pick, keys, values):
    cached = pl.BlockSpec((1, TOK, HEADS_STEP * HD), lambda i, pick: (pick[1], 0, i))
    return pl.pallas_call(
        pack_window_kernel,
        grid_spec=pltpu.PrefetchScalarGridSpec(
            num_scalar_prefetch=1,
            grid=(HEADS // HEADS_STEP,),
            in_specs=[cached] * 2,
            out_specs=pl.BlockSpec((HEADS_STEP, 2 * TOK, HD), lambda i, pick: (i, 0, 0)),
        ),
        out_shape=jax.ShapeDtypeStruct((HEADS, 2 * TOK, HD), BF16),
        compiler_params=params(60),
        name="pack_window",
    )(pick, keys, values)


def key_blocks(ref, step):
    sources, rows = ref.shape[0], ref.shape[1]
    return [
        ref[j : j + step].reshape(step * rows, HD) for j in range(0, sources, step)
    ]


def score(k, q):
    return lax.dot_general(k, q, (((1,), (1,)), ((), ())), preferred_element_type=F32)


def mix(v, raised):
    return lax.dot_general(
        v, raised.astype(BF16), (((0,), (0,)), ((), ())), preferred_element_type=F32
    )


def fold_rows(x):
    return jnp.sum(x.reshape(x.shape[0] // 8, 8, x.shape[1]), axis=0)


def attend_bounded(q, k_ref, v_ref, step, totals, acc):
    keys, values = key_blocks(k_ref, step), key_blocks(v_ref, step)
    following = score(keys[0], q)
    for j in range(len(keys)):
        scores = following
        if j + 1 < len(keys):
            following = score(keys[j + 1], q)
        raised = jnp.exp2(scores * SCALE)
        mixed, total = mix(values[j], raised), fold_rows(raised)
        acc = mixed if acc is None else acc + mixed
        totals = total if totals is None else totals + total
    return totals, acc


def attend_any(q, k_ref, v_ref, step, top_ref, totals_ref, acc_ref):
    sources, rows = k_ref.shape[0], k_ref.shape[1]

    def body(j, carry):
        here = pl.ds(j * step, step)
        scores = score(k_ref[here].reshape(step * rows, HD), q)
        before = top_ref[0:1, :]
        top = jnp.maximum(before, jnp.max(scores, axis=0, keepdims=True))
        raised = jnp.exp2((scores - top) * SCALE)
        fade = jnp.exp2((before - top) * SCALE)
        mixed = mix(v_ref[here].reshape(step * rows, HD), raised)
        acc_ref[...] = acc_ref[...] * fade + mixed
        totals_ref[...] = totals_ref[...] * fade + fold_rows(raised)
        top_ref[...] = jnp.broadcast_to(top, top_ref.shape)
        return carry

    lax.fori_loop(0, sources // step, body, 0)


def bounded(q, k_ref):
    widest = jnp.max(jnp.abs(k_ref[...].reshape(-1, HD)), axis=0, keepdims=True)
    reach = lax.dot_general(
        jnp.broadcast_to(widest, (16, HD)),
        jnp.abs(q),
        (((1,), (1,)), ((), ())),
        preferred_element_type=F32,
    )
    return jnp.max(reach) * (1.01 * SCALE) <= LIMIT


def attend_first_kernel(q_ref, k_ref, v_ref, slow_ref, top_ref, totals_ref, acc_ref):
    q = q_ref[...].reshape(BQ, HD)
    fits = bounded(q, k_ref)
    top_ref[...] = jnp.zeros(top_ref.shape, F32)
    totals_ref[...], acc_ref[...] = attend_bounded(q, k_ref, v_ref, 8, None, None)
    slow_ref[pl.program_id(0)] = jnp.where(fits, 0, 1)

    @pl.when(jnp.logical_not(fits))
    def _():
        top_ref[...] = jnp.full(top_ref.shape, -1e30, F32)
        totals_ref[...] = jnp.zeros(totals_ref.shape, F32)
        acc_ref[...] = jnp.zeros(acc_ref.shape, F32)
        attend_any(q, k_ref, v_ref, 4, top_ref, totals_ref, acc_ref)


def attend_last_kernel(
    q_ref, k_ref, v_ref, slow_ref, top_in_ref, totals_in_ref, acc_in_ref, weight_ref,
    out_ref, top_ref, totals_ref, acc_ref,
):
    q = q_ref[...].reshape(BQ, HD)
    fits = bounded(q, k_ref) & (slow_ref[pl.program_id(0)] == 0)
    totals_ref[...], acc_ref[...] = attend_bounded(
        q, k_ref, v_ref, 8, totals_in_ref[...], acc_in_ref[...]
    )

    @pl.when(jnp.logical_not(fits))
    def _():
        top_ref[...] = top_in_ref[...]
        totals_ref[...] = totals_in_ref[...]
        acc_ref[...] = acc_in_ref[...]
        attend_any(q, k_ref, v_ref, 8, top_ref, totals_ref, acc_ref)

    totals = jnp.sum(totals_ref[...], axis=0, keepdims=True)
    attended = (acc_ref[...] / totals).astype(BF16)
    moved = lax.dot_general(
        weight_ref[...], attended, (((0,), (0,)), ((), ())), preferred_element_type=F32
    )
    wide = attended.astype(F32)
    squares = jnp.broadcast_to(jnp.sum(wide * wide, axis=0, keepdims=True), (8, BQ))
    block = jnp.concatenate([moved, squares], axis=0).astype(BF16)
    for dest in range(BQ // TOK):
        out_ref[dest] = block[:, dest * TOK : (dest + 1) * TOK]


def attend(kind, queries, keys_values, k_rows, state=(), weight=None):
    total = HEADS * TOK
    blocks = BQ // TOK
    steps = total // BQ
    q_spec = pl.BlockSpec((blocks, TOK, HD), lambda i: (i, 3, 0))
    k_spec = pl.BlockSpec((HEADS, k_rows, HD), lambda i: (0, 0, 0))
    v_spec = pl.BlockSpec((HEADS, k_rows, HD), lambda i: (0, 1, 0))
    state_specs = [
        pl.BlockSpec(memory_space=pltpu.SMEM),
        pl.BlockSpec((8, BQ), lambda i: (0, i)),
        pl.BlockSpec((8, BQ), lambda i: (0, i)),
        pl.BlockSpec((HD, BQ), lambda i: (0, i)),
    ]
    state_shapes = [
        jax.ShapeDtypeStruct((steps,), jnp.int32),
        jax.ShapeDtypeStruct((8, total), F32),
        jax.ShapeDtypeStruct((8, total), F32),
        jax.ShapeDtypeStruct((HD, total), F32),
    ]
    in_specs = [q_spec, k_spec, v_spec]
    scratch = []
    args = (queries, keys_values, keys_values)
    if kind == "first":
        body, out_specs, out_shape = attend_first_kernel, state_specs, state_shapes
    else:
        body = attend_last_kernel
        in_specs += state_specs + [pl.BlockSpec(weight.shape, lambda i: (0, 0))]
        args += (*state, weight)
        out_specs = pl.BlockSpec((blocks, 72, HD), lambda i: (i, 0, 0))
        out_shape = jax.ShapeDtypeStruct((HEADS, 72, HD), BF16)
        scratch = [
            pltpu.VMEM((8, BQ), F32),
            pltpu.VMEM((8, BQ), F32),
            pltpu.VMEM((HD, BQ), F32),
        ]
    keys = HEADS * k_rows
    return pl.pallas_call(
        body,
        grid=(steps,),
        in_specs=in_specs,
        out_specs=out_specs,
        out_shape=out_shape,
        scratch_shapes=scratch,
        compiler_params=params(60),
        cost_estimate=pl.CostEstimate(
            flops=6 * total * keys * HD,
            transcendentals=total * keys,
            bytes_accessed=8 << 20,
        ),
        name="attend_" + kind,
    )(*args)


def clean_kernel(owner_ref, parts_ref, noisy_ref, prev_ref, out_ref, token_ref):
    width = HEADS * HD
    sums = jnp.sum(parts_ref[...].astype(F32), axis=0)
    scale = 1.0 / jnp.sqrt(sums[64:65] * (1.0 / width) + 1e-06)
    velocity = sums[0:64] * scale
    velocity = jnp.concatenate([velocity, jnp.zeros((64, HD), F32)], axis=0)
    token_ref[...] = jnp.transpose(velocity)
    lane = lax.broadcasted_iota(jnp.int32, (32, HD), 1)
    clean = []
    by_px = [token_ref[pl.ds(px, 32, stride=4), :] for px in range(4)]
    for i in range(2):
        moved = jnp.zeros((32, HD), F32)
        for px in range(4):
            turn = (px - i) * 32 % HD
            piece = pltpu.roll(by_px[px], turn, axis=1) if turn else by_px[px]
            moved = jnp.where(lane // 32 == px, piece, moved)
        clean.append(noisy_ref[i * 32 : i * 32 + 32, :].astype(F32) - moved)
    prev = prev_ref[...].astype(F32)
    owners = [owner_ref[t] for t in range(4)]
    ranks = []
    for t in range(4):
        rank = jnp.int32(0)
        for earlier in range(t):
            rank = rank + jnp.where(owners[earlier] == owners[t], 1, 0)
        ranks.append(rank)
    zero = jnp.zeros((8, HD), F32)
    for owner in range(4):
        rows = []
        for slot in range(2):
            picked = [zero] * 5
            for t in range(4):
                here = (owners[t] == owner) & (ranks[t] == slot)
                piece = slice(t * 8, t * 8 + 8)
                pieces = (
                    prev[0:32][piece],
                    prev[32:64][piece],
                    clean[0][piece],
                    clean[1][piece],
                    jnp.ones((8, HD), F32),
                )
                picked = [jnp.where(here, new, old) for new, old in zip(pieces, picked)]
            rows += picked
        out_ref[owner] = jnp.concatenate(rows, axis=0).astype(BF16)


def clean_and_place(owner, parts, noisy, prev):
    vmem = pl.BlockSpec(memory_space=pltpu.VMEM)
    return pl.pallas_call(
        clean_kernel,
        in_specs=[pl.BlockSpec(memory_space=pltpu.SMEM), vmem, vmem, vmem],
        out_specs=vmem,
        out_shape=jax.ShapeDtypeStruct((4, 80, HD), BF16),
        scratch_shapes=[pltpu.VMEM((HD, HD), F32)],
        compiler_params=pltpu.CompilerParams(vmem_limit_bytes=16 << 20),
        name="clean_and_place",
    )(owner, parts, noisy, prev)


def shift_rows(x, by):
    moved = pltpu.roll(x, by % 8, axis=1)
    y = lax.broadcasted_iota(jnp.int32, x.shape, 1)
    return jnp.where((y >= by) if by > 0 else (y < 8 + by), moved, 0.0)


def decode_kernel(
    mine_ref, in_ref, w_in_ref, b_in_ref, w_out_ref, b_out_ref, out_ref, latent_ref, part_ref, wide_ref
):
    tiles = 8
    flags = []
    for tile in range(tiles):
        block = in_ref[tile // 2, mine_ref[0], (tile % 2) * 40 : (tile % 2) * 40 + 40, :].astype(F32)
        for frames in range(2):
            for i in range(2):
                at = frames * 16 + i * 8
                latent_ref[pl.ds(tile * 32 + frames * 16 + i, 8, stride=2), :] = block[at : at + 8]
        flags.append(block[32:33])
    latent = latent_ref[...].reshape(tiles * 4, 8, HD)
    by_row = [shift_rows(latent, 1), latent, shift_rows(latent, -1)]
    by_row = [x.reshape(tiles * 32, HD) for x in by_row]
    lane = lax.broadcasted_iota(jnp.int32, (tiles * 32, HD), 1)
    low = lane < 64
    hidden = []
    for x in range(8):
        turn = (16 - 16 * x) % HD
        pair = [
            pltpu.roll(by_row[0], turn, axis=1) if turn else by_row[0],
            pltpu.roll(by_row[1], (turn + 64) % HD, axis=1) if turn != 64 else by_row[1],
            pltpu.roll(by_row[2], turn, axis=1) if turn else by_row[2],
        ]
        left = jnp.where(low, pair[0], pair[1])
        right = jnp.where(low, pair[2], 0.0)
        if x == 0:
            keep = (lane & 63) >= 16
            left, right = jnp.where(keep, left, 0.0), jnp.where(keep, right, 0.0)
        if x == 7:
            keep = (lane & 63) < 32
            left, right = jnp.where(keep, left, 0.0), jnp.where(keep, right, 0.0)
        taps = jnp.concatenate([left, right], axis=1).reshape(tiles, 4, 8, 2 * HD)
        columns = jnp.concatenate(
            [taps[:, dt : dt + 2].reshape(TOK, 2 * HD).astype(BF16) for dt in range(3)], axis=1
        )
        mid = jnp.dot(columns, w_in_ref[...], preferred_element_type=F32) + b_in_ref[...]
        hidden.append(mid / (1.0 + jnp.exp(-mid)))
    bias = b_out_ref[...]
    for a in range(2):
        for x in range(8):
            here = hidden[x]
            grouped = here.reshape(16, 8, 512)
            other = shift_rows(grouped, 1 if a == 0 else -1).reshape(TOK, 512)
            pair = [other, here] if a == 0 else [here, other]
            rows = jnp.concatenate([p.astype(BF16) for p in pair], axis=1)
            part_ref[x * TOK : (x + 1) * TOK, :] = jnp.dot(
                rows, w_out_ref[a], preferred_element_type=F32
            )
        for x in range(8):
            at = x * TOK
            first = part_ref[at : at + TOK, 128:256] + bias
            if x > 0:
                first = first + part_ref[at - TOK : at, 0:128]
            second = part_ref[at : at + TOK, 256:384] + bias
            if x < 7:
                second = second + part_ref[at + TOK : at + 2 * TOK, 384:512]
            wide_ref[pl.ds(a * 16 + 2 * x, TOK, stride=32), :] = first
            wide_ref[pl.ds(a * 16 + 2 * x + 1, TOK, stride=32), :] = second
    for tile in range(tiles):
        rows = slice(tile * 512, tile * 512 + 512)
        out_ref[rows, :] = jnp.where(flags[tile] > 0.5, wide_ref[rows, :], 0.0).astype(BF16)


def decode(mine, arrived, w_in, b_in, w_out, b_out):
    vmem = pl.BlockSpec(memory_space=pltpu.VMEM)
    return pl.pallas_call(
        decode_kernel,
        in_specs=[pl.BlockSpec(memory_space=pltpu.SMEM)] + [vmem] * 5,
        out_specs=vmem,
        out_shape=jax.ShapeDtypeStruct((8 * 512, HD), BF16),
        scratch_shapes=[
            pltpu.VMEM((256, HD), F32),
            pltpu.VMEM((8 * TOK, 512), F32),
            pltpu.VMEM((8 * 512, HD), F32),
        ],
        compiler_params=pltpu.CompilerParams(vmem_limit_bytes=48 << 20),
        name="decode",
    )(mine, arrived, w_in, b_in, w_out, b_out)


def head_weight(velocity_weight):
    head = lax.axis_index("ctx")
    return lax.dynamic_slice_in_dim(velocity_weight, head * HD, HD, 0)


def place_in_weight(weight):
    split = weight.reshape(3, 3, 48, 512)
    return jnp.pad(split, ((0, 0), (0, 1), (0, 16), (0, 0))).reshape(3 * 4 * 64, 512)


def place_out_weight(weight):
    w = weight.reshape(3, 3, 512, 128).astype(F32)
    rows = [[w[0], w[1] + w[2]], [w[0] + w[1], w[2]]]
    phases = []
    for a in range(2):
        halves = []
        for r in rows[a]:
            halves.append(jnp.concatenate([r[0], r[1] + r[2], r[0] + r[1], r[2]], axis=1))
        phases.append(jnp.concatenate(halves, axis=0))
    return jnp.stack(phases).astype(BF16)


def latent_rows(latent):
    return latent.reshape(4, 2, 4, 2, HD).transpose(3, 0, 1, 2, 4).reshape(64, HD)


def exchange(x, axis):
    return lax.all_to_all(x, axis, split_axis=0, concat_axis=0, tiled=True)


def local(
    clip_queries,
    clip_keys,
    clip_values,
    cache_keys,
    cache_values,
    clip_pick,
    noisy_latent,
    prev_latent,
    velocity_weight,
    tile_owner,
    conv_in_weight,
    conv_in_bias,
    conv_out_weight,
    conv_out_bias,
):
    pick = clip_pick[0]
    current = (clip_queries[0], clip_keys[0], clip_values[0])
    clip = exchange(pack_first(pick, current, cache_keys[0], cache_values[0]), "ctx")
    window = pack_window(pick, cache_keys[0], cache_values[0])
    weight = head_weight(velocity_weight)
    w_in = place_in_weight(conv_in_weight)
    w_out = place_out_weight(conv_out_weight)
    noisy = latent_rows(noisy_latent[0])
    prev = latent_rows(prev_latent[0])

    clip, window, weight, w_in, w_out, noisy, prev = lax.optimization_barrier(
        (clip, window, weight, w_in, w_out, noisy, prev)
    )
    window = exchange(window, "ctx")
    state = attend("first", clip, clip, 192)
    parts = attend("last", clip, window, TOK, state, weight)
    parts = exchange(parts, "ctx")
    outgoing = clean_and_place(tile_owner[0], parts, noisy, prev)
    arrived = lax.all_gather(outgoing, "grp", axis=0)
    mine = lax.axis_index("grp").reshape(1)
    decoded = decode(
        mine, arrived, w_in, conv_in_bias.reshape(1, -1), w_out, conv_out_bias.reshape(1, -1)
    )
    return decoded.reshape(1, 1, 4, 2, 2, 256, 128)


def solution(mesh):
    in_specs = (
        P("grp", "ctx", None),
        P("grp", "ctx", None),
        P("grp", "ctx", None),
        P("grp", None, "ctx", None),
        P("grp", None, "ctx", None),
        P("grp", None),
        P("grp", "ctx", None, None),
        P("grp", "ctx", None, None),
        P(),
        P("grp", "ctx"),
        P(),
        P(),
        P(),
        P(),
    )
    out_specs = P("grp", "ctx", None, None, None, None, None)
    return jax.shard_map(local, mesh=mesh, in_specs=in_specs, out_specs=out_specs, check_vma=False)
```

```python
import math

import jax
import jax.numpy as jnp
from jax import lax
from jax.experimental import pallas as pl
from jax.experimental.pallas import tpu as pltpu
from jax.sharding import PartitionSpec as P

HEADS = 32
HD = 128
TOK = 128
F32 = jnp.float32
BF16 = jnp.bfloat16
SCALE = math.log2(math.e) / math.sqrt(HD)
HEADS_STEP = 8
BQ = 2048
LIMIT = 110.0


def params(mib, axes=1):
    return pltpu.CompilerParams(
        vmem_limit_bytes=mib << 20, dimension_semantics=("arbitrary",) * axes
    )


def pack_first_kernel(pick_ref, q_ref, k_ref, v_ref, sink_k_ref, sink_v_ref, out_ref):
    for head in range(out_ref.shape[0]):
        lanes = slice(head * HD, (head + 1) * HD)
        out_ref[head, 0:TOK, :] = k_ref[:, lanes]
        out_ref[head, 192 : 192 + TOK, :] = v_ref[:, lanes]
        out_ref[head, 384 : 384 + TOK, :] = q_ref[:, lanes]
        for tile in range(4):
            rows = slice(tile * 32, tile * 32 + 16)
            at = TOK + tile * 16
            out_ref[head, at : at + 16, :] = sink_k_ref[0, rows, lanes]
            out_ref[head, 192 + at : 208 + at, :] = sink_v_ref[0, rows, lanes]


def pack_first(pick, current, keys, values):
    heads = 2 * HEADS_STEP
    own = pl.BlockSpec((TOK, heads * HD), lambda i, pick: (0, i))
    cached = pl.BlockSpec((1, TOK, heads * HD), lambda i, pick: (pick[0], 0, i))
    return pl.pallas_call(
        pack_first_kernel,
        grid_spec=pltpu.PrefetchScalarGridSpec(
            num_scalar_prefetch=1,
            grid=(HEADS // heads,),
            in_specs=[own] * 3 + [cached] * 2,
            out_specs=pl.BlockSpec((heads, 4 * TOK, HD), lambda i, pick: (i, 0, 0)),
        ),
        out_shape=jax.ShapeDtypeStruct((HEADS, 4 * TOK, HD), BF16),
        compiler_params=params(60),
        name="pack_first",
    )(pick, *current, keys, values)


def pack_window_kernel(pick_ref, k_ref, v_ref, out_ref):
    for head in range(HEADS_STEP):
        lanes = slice(head * HD, (head + 1) * HD)
        out_ref[head, 0:TOK, :] = k_ref[0, :, lanes]
        out_ref[head, TOK : 2 * TOK, :] = v_ref[0, :, lanes]


def pack_window(pick, keys, values):
    cached = pl.BlockSpec((1, TOK, HEADS_STEP * HD), lambda i, pick: (pick[1], 0, i))
    return pl.pallas_call(
        pack_window_kernel,
        grid_spec=pltpu.PrefetchScalarGridSpec(
            num_scalar_prefetch=1,
            grid=(HEADS // HEADS_STEP,),
            in_specs=[cached] * 2,
            out_specs=pl.BlockSpec((HEADS_STEP, 2 * TOK, HD), lambda i, pick: (i, 0, 0)),
        ),
        out_shape=jax.ShapeDtypeStruct((HEADS, 2 * TOK, HD), BF16),
        compiler_params=params(60),
        name="pack_window",
    )(pick, keys, values)


def key_blocks(ref, step):
    sources, rows = ref.shape[0], ref.shape[1]
    return [
        ref[j : j + step].reshape(step * rows, HD) for j in range(0, sources, step)
    ]


def score(k, q):
    return lax.dot_general(k, q, (((1,), (1,)), ((), ())), preferred_element_type=F32)


def mix(v, raised):
    return lax.dot_general(
        v, raised.astype(BF16), (((0,), (0,)), ((), ())), preferred_element_type=F32
    )


def fold_rows(x):
    return jnp.sum(x.reshape(x.shape[0] // 8, 8, x.shape[1]), axis=0)


def attend_bounded(q, k_ref, v_ref, step, totals, acc):
    keys, values = key_blocks(k_ref, step), key_blocks(v_ref, step)
    following = score(keys[0], q)
    for j in range(len(keys)):
        scores = following
        if j + 1 < len(keys):
            following = score(keys[j + 1], q)
        raised = jnp.exp2(scores * SCALE)
        mixed, total = mix(values[j], raised), fold_rows(raised)
        acc = mixed if acc is None else acc + mixed
        totals = total if totals is None else totals + total
    return totals, acc


def attend_any(q, k_ref, v_ref, step, top_ref, totals_ref, acc_ref):
    sources, rows = k_ref.shape[0], k_ref.shape[1]

    def body(j, carry):
        here = pl.ds(j * step, step)
        scores = score(k_ref[here].reshape(step * rows, HD), q)
        before = top_ref[0:1, :]
        top = jnp.maximum(before, jnp.max(scores, axis=0, keepdims=True))
        raised = jnp.exp2((scores - top) * SCALE)
        fade = jnp.exp2((before - top) * SCALE)
        mixed = mix(v_ref[here].reshape(step * rows, HD), raised)
        acc_ref[...] = acc_ref[...] * fade + mixed
        totals_ref[...] = totals_ref[...] * fade + fold_rows(raised)
        top_ref[...] = jnp.broadcast_to(top, top_ref.shape)
        return carry

    lax.fori_loop(0, sources // step, body, 0)


def bounded(q, k_ref):
    widest = jnp.max(jnp.abs(k_ref[...].reshape(-1, HD)), axis=0, keepdims=True)
    reach = lax.dot_general(
        jnp.broadcast_to(widest, (16, HD)),
        jnp.abs(q),
        (((1,), (1,)), ((), ())),
        preferred_element_type=F32,
    )
    return jnp.max(reach) * (1.01 * SCALE) <= LIMIT


def attend_first_kernel(q_ref, k_ref, v_ref, slow_ref, top_ref, totals_ref, acc_ref):
    q = q_ref[...].reshape(BQ, HD)
    fits = bounded(q, k_ref)
    top_ref[...] = jnp.zeros(top_ref.shape, F32)
    totals_ref[...], acc_ref[...] = attend_bounded(q, k_ref, v_ref, 8, None, None)
    slow_ref[pl.program_id(0)] = jnp.where(fits, 0, 1)

    @pl.when(jnp.logical_not(fits))
    def _():
        top_ref[...] = jnp.full(top_ref.shape, -1e30, F32)
        totals_ref[...] = jnp.zeros(totals_ref.shape, F32)
        acc_ref[...] = jnp.zeros(acc_ref.shape, F32)
        attend_any(q, k_ref, v_ref, 4, top_ref, totals_ref, acc_ref)


def attend_last_kernel(
    q_ref, k_ref, v_ref, slow_ref, top_in_ref, totals_in_ref, acc_in_ref, weight_ref,
    out_ref, top_ref, totals_ref, acc_ref,
):
    q = q_ref[...].reshape(BQ, HD)
    fits = bounded(q, k_ref) & (slow_ref[pl.program_id(0)] == 0)
    totals_ref[...], acc_ref[...] = attend_bounded(
        q, k_ref, v_ref, 8, totals_in_ref[...], acc_in_ref[...]
    )

    @pl.when(jnp.logical_not(fits))
    def _():
        top_ref[...] = top_in_ref[...]
        totals_ref[...] = totals_in_ref[...]
        acc_ref[...] = acc_in_ref[...]
        attend_any(q, k_ref, v_ref, 8, top_ref, totals_ref, acc_ref)

    totals = jnp.sum(totals_ref[...], axis=0, keepdims=True)
    attended = (acc_ref[...] / totals).astype(BF16)
    moved = lax.dot_general(
        weight_ref[...], attended, (((0,), (0,)), ((), ())), preferred_element_type=F32
    )
    wide = attended.astype(F32)
    squares = jnp.broadcast_to(jnp.sum(wide * wide, axis=0, keepdims=True), (8, BQ))
    block = jnp.concatenate([moved, squares], axis=0).astype(BF16)
    for dest in range(BQ // TOK):
        out_ref[dest] = block[:, dest * TOK : (dest + 1) * TOK]


def attend(kind, queries, keys_values, k_rows, state=(), weight=None):
    total = HEADS * TOK
    blocks = BQ // TOK
    steps = total // BQ
    q_spec = pl.BlockSpec((blocks, TOK, HD), lambda i: (i, 3, 0))
    k_spec = pl.BlockSpec((HEADS, k_rows, HD), lambda i: (0, 0, 0))
    v_spec = pl.BlockSpec((HEADS, k_rows, HD), lambda i: (0, 1, 0))
    state_specs = [
        pl.BlockSpec(memory_space=pltpu.SMEM),
        pl.BlockSpec((8, BQ), lambda i: (0, i)),
        pl.BlockSpec((8, BQ), lambda i: (0, i)),
        pl.BlockSpec((HD, BQ), lambda i: (0, i)),
    ]
    state_shapes = [
        jax.ShapeDtypeStruct((steps,), jnp.int32),
        jax.ShapeDtypeStruct((8, total), F32),
        jax.ShapeDtypeStruct((8, total), F32),
        jax.ShapeDtypeStruct((HD, total), F32),
    ]
    in_specs = [q_spec, k_spec, v_spec]
    scratch = []
    args = (queries, keys_values, keys_values)
    if kind == "first":
        body, out_specs, out_shape = attend_first_kernel, state_specs, state_shapes
    else:
        body = attend_last_kernel
        in_specs += state_specs + [pl.BlockSpec(weight.shape, lambda i: (0, 0))]
        args += (*state, weight)
        out_specs = pl.BlockSpec((blocks, 72, HD), lambda i: (i, 0, 0))
        out_shape = jax.ShapeDtypeStruct((HEADS, 72, HD), BF16)
        scratch = [
            pltpu.VMEM((8, BQ), F32),
            pltpu.VMEM((8, BQ), F32),
            pltpu.VMEM((HD, BQ), F32),
        ]
    keys = HEADS * k_rows
    return pl.pallas_call(
        body,
        grid=(steps,),
        in_specs=in_specs,
        out_specs=out_specs,
        out_shape=out_shape,
        scratch_shapes=scratch,
        compiler_params=params(60),
        cost_estimate=pl.CostEstimate(
            flops=6 * total * keys * HD,
            transcendentals=total * keys,
            bytes_accessed=8 << 20,
        ),
        name="attend_" + kind,
    )(*args)


def clean_kernel(parts_ref, noisy_ref, out_ref, token_ref):
    width = HEADS * HD
    sums = jnp.sum(parts_ref[...].astype(F32), axis=0)
    scale = 1.0 / jnp.sqrt(sums[64:65] * (1.0 / width) + 1e-06)
    velocity = sums[0:64] * scale
    velocity = jnp.concatenate([velocity, jnp.zeros((64, HD), F32)], axis=0)
    token_ref[...] = jnp.transpose(velocity)
    lane = lax.broadcasted_iota(jnp.int32, (32, HD), 1)
    by_px = [token_ref[pl.ds(px, 32, stride=4), :] for px in range(4)]
    for i in range(2):
        moved = jnp.zeros((32, HD), F32)
        for px in range(4):
            turn = (px - i) * 32 % HD
            piece = pltpu.roll(by_px[px], turn, axis=1) if turn else by_px[px]
            moved = jnp.where(lane // 32 == px, piece, moved)
        rows = slice(i * 32, i * 32 + 32)
        out_ref[rows, :] = (noisy_ref[rows, :].astype(F32) - moved).astype(BF16)


def clean_rows(parts, noisy):
    vmem = pl.BlockSpec(memory_space=pltpu.VMEM)
    return pl.pallas_call(
        clean_kernel,
        in_specs=[vmem, vmem],
        out_specs=vmem,
        out_shape=jax.ShapeDtypeStruct((64, HD), BF16),
        scratch_shapes=[pltpu.VMEM((HD, HD), F32)],
        compiler_params=pltpu.CompilerParams(vmem_limit_bytes=16 << 20),
        name="clean_rows",
    )(parts, noisy)


def shift_rows(x, by):
    moved = pltpu.roll(x, by % 8, axis=1)
    y = lax.broadcasted_iota(jnp.int32, x.shape, 1)
    return jnp.where((y >= by) if by > 0 else (y < 8 + by), moved, 0.0)


def decode_kernel(
    mine_ref, prev_ref, clean_ref, w_in_ref, b_in_ref, w_out_ref, b_out_ref,
    out_ref, latent_ref, column_ref, part_ref, wide_ref,
):
    tiles = 8
    mine = mine_ref[0].astype(F32)
    flags = []
    for sender in range(4):
        old = prev_ref[sender].astype(F32)
        new = clean_ref[sender].astype(F32)
        owners = [old[64 + t : 65 + t] for t in range(4)]
        ranks = []
        for t in range(4):
            rank = jnp.zeros((1, HD), F32)
            for earlier in range(t):
                rank = rank + jnp.where(owners[earlier] == owners[t], 1.0, 0.0)
            ranks.append(rank)
        for slot in range(2):
            here = [
                jnp.where((owners[t] == mine) & (ranks[t] == slot), 1.0, 0.0) for t in range(4)
            ]
            flags.append(here[0] + here[1] + here[2] + here[3])
            masks = [jnp.broadcast_to(h, (8, HD)) > 0.5 for h in here]
            tile = sender * 2 + slot
            for frames, source in ((0, old), (1, new)):
                for i in range(2):
                    picked = jnp.zeros((8, HD), F32)
                    for t in range(4):
                        at = i * 32 + t * 8
                        picked = jnp.where(masks[t], source[at : at + 8], picked)
                    latent_ref[pl.ds(tile * 32 + frames * 16 + i, 8, stride=2), :] = picked
    latent = latent_ref[...].reshape(tiles * 4, 8, HD)
    by_row = [shift_rows(latent, 1), latent, shift_rows(latent, -1)]
    by_row = [x.reshape(tiles * 32, HD) for x in by_row]
    lane = lax.broadcasted_iota(jnp.int32, (tiles * 32, HD), 1)
    low = lane < 64
    for x in range(8):
        turn = (16 - 16 * x) % HD
        pair = [
            pltpu.roll(by_row[0], turn, axis=1) if turn else by_row[0],
            pltpu.roll(by_row[1], (turn + 64) % HD, axis=1) if turn != 64 else by_row[1],
            pltpu.roll(by_row[2], turn, axis=1) if turn else by_row[2],
        ]
        left = jnp.where(low, pair[0], pair[1])
        right = jnp.where(low, pair[2], 0.0)
        if x == 0:
            keep = (lane & 63) >= 16
            left, right = jnp.where(keep, left, 0.0), jnp.where(keep, right, 0.0)
        if x == 7:
            keep = (lane & 63) < 32
            left, right = jnp.where(keep, left, 0.0), jnp.where(keep, right, 0.0)
        taps = jnp.concatenate([left, right], axis=1).reshape(tiles, 4, 8, 2 * HD)
        columns = jnp.concatenate(
            [taps[:, dt : dt + 2].reshape(TOK, 2 * HD).astype(BF16) for dt in range(3)], axis=1
        )
        column_ref[x * TOK : (x + 1) * TOK, :] = columns
    mid = jnp.dot(column_ref[...], w_in_ref[...], preferred_element_type=F32) + b_in_ref[...]
    hidden = mid / (1.0 + jnp.exp(-mid))
    grouped = hidden.reshape(8 * TOK // 8, 8, 512)
    here = hidden.astype(BF16)
    bias = b_out_ref[...]
    for a in range(2):
        other = shift_rows(grouped, 1 if a == 0 else -1).reshape(8 * TOK, 512).astype(BF16)
        rows = jnp.concatenate([other, here] if a == 0 else [here, other], axis=1)
        part_ref[...] = jnp.dot(rows, w_out_ref[a], preferred_element_type=F32)
        for x in range(8):
            at = x * TOK
            first = part_ref[at : at + TOK, 128:256] + bias
            if x > 0:
                first = first + part_ref[at - TOK : at, 0:128]
            second = part_ref[at : at + TOK, 256:384] + bias
            if x < 7:
                second = second + part_ref[at + TOK : at + 2 * TOK, 384:512]
            wide_ref[pl.ds(a * 16 + 2 * x, TOK, stride=32), :] = first
            wide_ref[pl.ds(a * 16 + 2 * x + 1, TOK, stride=32), :] = second
    for tile in range(tiles):
        rows = slice(tile * 512, tile * 512 + 512)
        out_ref[rows, :] = jnp.where(flags[tile] > 0.5, wide_ref[rows, :], 0.0).astype(BF16)


def decode(mine, prev, clean, w_in, b_in, w_out, b_out):
    vmem = pl.BlockSpec(memory_space=pltpu.VMEM)
    return pl.pallas_call(
        decode_kernel,
        in_specs=[pl.BlockSpec(memory_space=pltpu.SMEM)] + [vmem] * 6,
        out_specs=vmem,
        out_shape=jax.ShapeDtypeStruct((8 * 512, HD), BF16),
        scratch_shapes=[
            pltpu.VMEM((256, HD), F32),
            pltpu.VMEM((8 * TOK, 768), BF16),
            pltpu.VMEM((8 * TOK, 512), F32),
            pltpu.VMEM((8 * 512, HD), F32),
        ],
        compiler_params=pltpu.CompilerParams(vmem_limit_bytes=48 << 20),
        name="decode",
    )(mine, prev, clean, w_in, b_in, w_out, b_out)


def head_weight(velocity_weight):
    head = lax.axis_index("ctx")
    return lax.dynamic_slice_in_dim(velocity_weight, head * HD, HD, 0)


def place_in_weight(weight):
    split = weight.reshape(3, 3, 48, 512)
    return jnp.pad(split, ((0, 0), (0, 1), (0, 16), (0, 0))).reshape(3 * 4 * 64, 512)


def place_out_weight(weight):
    w = weight.reshape(3, 3, 512, 128).astype(F32)
    rows = [[w[0], w[1] + w[2]], [w[0] + w[1], w[2]]]
    phases = []
    for a in range(2):
        halves = []
        for r in rows[a]:
            halves.append(jnp.concatenate([r[0], r[1] + r[2], r[0] + r[1], r[2]], axis=1))
        phases.append(jnp.concatenate(halves, axis=0))
    return jnp.stack(phases).astype(BF16)


def latent_rows(latent):
    return latent.reshape(4, 2, 4, 2, HD).transpose(3, 0, 1, 2, 4).reshape(64, HD)


def exchange(x, axis):
    return lax.all_to_all(x, axis, split_axis=0, concat_axis=0, tiled=True)


def local(
    clip_queries,
    clip_keys,
    clip_values,
    cache_keys,
    cache_values,
    clip_pick,
    noisy_latent,
    prev_latent,
    velocity_weight,
    tile_owner,
    conv_in_weight,
    conv_in_bias,
    conv_out_weight,
    conv_out_bias,
):
    pick = clip_pick[0]
    current = (clip_queries[0], clip_keys[0], clip_values[0])
    clip = exchange(pack_first(pick, current, cache_keys[0], cache_values[0]), "ctx")
    window = pack_window(pick, cache_keys[0], cache_values[0])
    weight = head_weight(velocity_weight)
    w_in = place_in_weight(conv_in_weight)
    w_out = place_out_weight(conv_out_weight)
    noisy = latent_rows(noisy_latent[0])
    owners = jnp.broadcast_to(tile_owner[0].astype(BF16)[:, None], (4, HD))
    owners = jnp.pad(owners, ((0, 4), (0, 0)))
    prev = jnp.concatenate([latent_rows(prev_latent[0]), owners], axis=0)
    prev = lax.all_gather(prev, "grp", axis=0)

    clip, window, weight, w_in, w_out, noisy, prev = lax.optimization_barrier(
        (clip, window, weight, w_in, w_out, noisy, prev)
    )
    window = exchange(window, "ctx")
    state = attend("first", clip, clip, 192)
    parts = attend("last", clip, window, TOK, state, weight)
    parts = exchange(parts, "ctx")
    clean = lax.all_gather(clean_rows(parts, noisy), "grp", axis=0)
    mine = lax.axis_index("grp").reshape(1)
    decoded = decode(
        mine, prev, clean, w_in, conv_in_bias.reshape(1, -1), w_out, conv_out_bias.reshape(1, -1)
    )
    return decoded.reshape(1, 1, 4, 2, 2, 256, 128)


def solution(mesh):
    in_specs = (
        P("grp", "ctx", None),
        P("grp", "ctx", None),
        P("grp", "ctx", None),
        P("grp", None, "ctx", None),
        P("grp", None, "ctx", None),
        P("grp", None),
        P("grp", "ctx", None, None),
        P("grp", "ctx", None, None),
        P(),
        P("grp", "ctx"),
        P(),
        P(),
        P(),
        P(),
    )
    out_specs = P("grp", "ctx", None, None, None, None, None)
    return jax.shard_map(local, mesh=mesh, in_specs=in_specs, out_specs=out_specs, check_vma=False)
```

```python
import math

import jax
import jax.numpy as jnp
from jax import lax
from jax.experimental import pallas as pl
from jax.experimental.pallas import tpu as pltpu
from jax.sharding import PartitionSpec as P

HEADS = 32
HD = 128
TOK = 128
F32 = jnp.float32
BF16 = jnp.bfloat16
SCALE = math.log2(math.e) / math.sqrt(HD)
HEADS_STEP = 8
BQ = 2048
LIMIT = 110.0
SPLIT = 4


def params(mib, axes=1):
    return pltpu.CompilerParams(
        vmem_limit_bytes=mib << 20, dimension_semantics=("arbitrary",) * axes
    )


def pack_first_kernel(pick_ref, q_ref, k_ref, v_ref, sink_k_ref, sink_v_ref, out_ref):
    for head in range(out_ref.shape[0]):
        lanes = slice(head * HD, (head + 1) * HD)
        out_ref[head, 0:TOK, :] = k_ref[:, lanes]
        out_ref[head, 192 : 192 + TOK, :] = v_ref[:, lanes]
        out_ref[head, 384 : 384 + TOK, :] = q_ref[:, lanes]
        for tile in range(4):
            rows = slice(tile * 32, tile * 32 + 16)
            at = TOK + tile * 16
            out_ref[head, at : at + 16, :] = sink_k_ref[0, rows, lanes]
            out_ref[head, 192 + at : 208 + at, :] = sink_v_ref[0, rows, lanes]


def pack_first(pick, current, keys, values):
    heads = 2 * HEADS_STEP
    own = pl.BlockSpec((TOK, heads * HD), lambda i, pick: (0, i))
    cached = pl.BlockSpec((1, TOK, heads * HD), lambda i, pick: (pick[0], 0, i))
    return pl.pallas_call(
        pack_first_kernel,
        grid_spec=pltpu.PrefetchScalarGridSpec(
            num_scalar_prefetch=1,
            grid=(HEADS // heads,),
            in_specs=[own] * 3 + [cached] * 2,
            out_specs=pl.BlockSpec((heads, 4 * TOK, HD), lambda i, pick: (i, 0, 0)),
        ),
        out_shape=jax.ShapeDtypeStruct((HEADS, 4 * TOK, HD), BF16),
        compiler_params=params(60),
        name="pack_first",
    )(pick, *current, keys, values)


def pack_window_kernel(pick_ref, k_ref, v_ref, out_ref):
    for head in range(HEADS_STEP):
        lanes = slice(head * HD, (head + 1) * HD)
        out_ref[head, 0:TOK, :] = k_ref[0, :, lanes]
        out_ref[head, TOK : 2 * TOK, :] = v_ref[0, :, lanes]


def pack_window(pick, keys, values):
    cached = pl.BlockSpec((1, TOK, HEADS_STEP * HD), lambda i, pick: (pick[1], 0, i))
    return pl.pallas_call(
        pack_window_kernel,
        grid_spec=pltpu.PrefetchScalarGridSpec(
            num_scalar_prefetch=1,
            grid=(HEADS // HEADS_STEP,),
            in_specs=[cached] * 2,
            out_specs=pl.BlockSpec((HEADS_STEP, 2 * TOK, HD), lambda i, pick: (i, 0, 0)),
        ),
        out_shape=jax.ShapeDtypeStruct((HEADS, 2 * TOK, HD), BF16),
        compiler_params=params(60),
        name="pack_window",
    )(pick, keys, values)


def key_blocks(refs, step):
    rows = refs[0].shape[1]
    return [
        ref[j : j + step].reshape(step * rows, HD)
        for ref in refs
        for j in range(0, ref.shape[0], step)
    ]


def score(k, q):
    return lax.dot_general(k, q, (((1,), (1,)), ((), ())), preferred_element_type=F32)


def mix(v, raised):
    return lax.dot_general(
        v, raised.astype(BF16), (((0,), (0,)), ((), ())), preferred_element_type=F32
    )


def fold_rows(x):
    return jnp.sum(x.reshape(x.shape[0] // 8, 8, x.shape[1]), axis=0)


def attend_bounded(q, k_refs, v_refs, step, totals, acc):
    keys, values = key_blocks(k_refs, step), key_blocks(v_refs, step)
    following = score(keys[0], q)
    for j in range(len(keys)):
        scores = following
        if j + 1 < len(keys):
            following = score(keys[j + 1], q)
        raised = jnp.exp2(scores * SCALE)
        mixed, total = mix(values[j], raised), fold_rows(raised)
        acc = mixed if acc is None else acc + mixed
        totals = total if totals is None else totals + total
    return totals, acc


def attend_any(q, k_refs, v_refs, step, top_ref, totals_ref, acc_ref):
    for k_ref, v_ref in zip(k_refs, v_refs):
        sources, rows = k_ref.shape[0], k_ref.shape[1]

        def body(j, carry, k_ref=k_ref, v_ref=v_ref, rows=rows):
            here = pl.ds(j * step, step)
            scores = score(k_ref[here].reshape(step * rows, HD), q)
            before = top_ref[0:1, :]
            top = jnp.maximum(before, jnp.max(scores, axis=0, keepdims=True))
            raised = jnp.exp2((scores - top) * SCALE)
            fade = jnp.exp2((before - top) * SCALE)
            mixed = mix(v_ref[here].reshape(step * rows, HD), raised)
            acc_ref[...] = acc_ref[...] * fade + mixed
            totals_ref[...] = totals_ref[...] * fade + fold_rows(raised)
            top_ref[...] = jnp.broadcast_to(top, top_ref.shape)
            return carry

        lax.fori_loop(0, sources // step, body, 0)


def bounded(q, k_refs):
    widest = [jnp.max(jnp.abs(k[...].reshape(-1, HD)), axis=0, keepdims=True) for k in k_refs]
    while len(widest) > 1:
        widest = [jnp.maximum(*widest[:2])] + widest[2:]
    widest = widest[0]
    reach = lax.dot_general(
        jnp.broadcast_to(widest, (16, HD)),
        jnp.abs(q),
        (((1,), (1,)), ((), ())),
        preferred_element_type=F32,
    )
    return jnp.max(reach) * (1.01 * SCALE) <= LIMIT


def attend_first_kernel(q_ref, *refs):
    k_refs, v_refs = refs[:SPLIT], refs[SPLIT : 2 * SPLIT]
    slow_ref, top_ref, totals_ref, acc_ref = refs[2 * SPLIT :]
    q = q_ref[...].reshape(BQ, HD)
    fits = bounded(q, k_refs)
    top_ref[...] = jnp.zeros(top_ref.shape, F32)
    totals_ref[...], acc_ref[...] = attend_bounded(q, k_refs, v_refs, 8, None, None)
    slow_ref[pl.program_id(0)] = jnp.where(fits, 0, 1)

    @pl.when(jnp.logical_not(fits))
    def _():
        top_ref[...] = jnp.full(top_ref.shape, -1e30, F32)
        totals_ref[...] = jnp.zeros(totals_ref.shape, F32)
        acc_ref[...] = jnp.zeros(acc_ref.shape, F32)
        attend_any(q, k_refs, v_refs, 4, top_ref, totals_ref, acc_ref)


def attend_last_kernel(q_ref, *refs):
    k_refs, v_refs = refs[:SPLIT], refs[SPLIT : 2 * SPLIT]
    slow_ref, top_in_ref, totals_in_ref, acc_in_ref, weight_ref = refs[2 * SPLIT : 2 * SPLIT + 5]
    out_ref, top_ref, totals_ref, acc_ref = refs[2 * SPLIT + 5 :]
    q = q_ref[...].reshape(BQ, HD)
    fits = bounded(q, k_refs) & (slow_ref[pl.program_id(0)] == 0)
    totals_ref[...], acc_ref[...] = attend_bounded(
        q, k_refs, v_refs, 8, totals_in_ref[...], acc_in_ref[...]
    )

    @pl.when(jnp.logical_not(fits))
    def _():
        top_ref[...] = top_in_ref[...]
        totals_ref[...] = totals_in_ref[...]
        acc_ref[...] = acc_in_ref[...]
        attend_any(q, k_refs, v_refs, 8, top_ref, totals_ref, acc_ref)

    totals = jnp.sum(totals_ref[...], axis=0, keepdims=True)
    attended = (acc_ref[...] / totals).astype(BF16)
    moved = lax.dot_general(
        weight_ref[...], attended, (((0,), (0,)), ((), ())), preferred_element_type=F32
    )
    wide = attended.astype(F32)
    squares = jnp.broadcast_to(jnp.sum(wide * wide, axis=0, keepdims=True), (8, BQ))
    block = jnp.concatenate([moved, squares], axis=0).astype(BF16)
    for dest in range(BQ // TOK):
        out_ref[dest] = block[:, dest * TOK : (dest + 1) * TOK]


def attend(kind, queries, keys_values, k_rows, state=(), weight=None):
    total = HEADS * TOK
    blocks = BQ // TOK
    steps = total // BQ
    q_spec = pl.BlockSpec((blocks, TOK, HD), lambda i: (i, 3, 0))
    kv_specs = [
        pl.BlockSpec((HEADS // SPLIT, k_rows, HD), lambda i, part=part, place=place: (part, place, 0))
        for place in range(2)
        for part in range(SPLIT)
    ]
    state_specs = [
        pl.BlockSpec(memory_space=pltpu.SMEM),
        pl.BlockSpec((8, BQ), lambda i: (0, i)),
        pl.BlockSpec((8, BQ), lambda i: (0, i)),
        pl.BlockSpec((HD, BQ), lambda i: (0, i)),
    ]
    state_shapes = [
        jax.ShapeDtypeStruct((steps,), jnp.int32),
        jax.ShapeDtypeStruct((8, total), F32),
        jax.ShapeDtypeStruct((8, total), F32),
        jax.ShapeDtypeStruct((HD, total), F32),
    ]
    in_specs = [q_spec] + kv_specs
    scratch = []
    args = (queries,) + (keys_values,) * (2 * SPLIT)
    if kind == "first":
        body, out_specs, out_shape = attend_first_kernel, state_specs, state_shapes
    else:
        body = attend_last_kernel
        in_specs += state_specs + [pl.BlockSpec(weight.shape, lambda i: (0, 0))]
        args += (*state, weight)
        out_specs = pl.BlockSpec((blocks, 72, HD), lambda i: (i, 0, 0))
        out_shape = jax.ShapeDtypeStruct((HEADS, 72, HD), BF16)
        scratch = [
            pltpu.VMEM((8, BQ), F32),
            pltpu.VMEM((8, BQ), F32),
            pltpu.VMEM((HD, BQ), F32),
        ]
    keys = HEADS * k_rows
    return pl.pallas_call(
        body,
        grid=(steps,),
        in_specs=in_specs,
        out_specs=out_specs,
        out_shape=out_shape,
        scratch_shapes=scratch,
        compiler_params=params(60),
        cost_estimate=pl.CostEstimate(
            flops=6 * total * keys * HD,
            transcendentals=total * keys,
            bytes_accessed=8 << 20,
        ),
        name="attend_" + kind,
    )(*args)


def clean_kernel(*refs):
    parts, (noisy_ref, prev_ref, out_ref, token_ref) = refs[:SPLIT], refs[SPLIT:]
    width = HEADS * HD
    sums = [jnp.sum(part[...].astype(F32), axis=0) for part in parts]
    sums = (sums[0] + sums[1]) + (sums[2] + sums[3])
    scale = 1.0 / jnp.sqrt(sums[64:65] * (1.0 / width) + 1e-06)
    velocity = sums[0:64] * scale
    velocity = jnp.concatenate([velocity, jnp.zeros((64, HD), F32)], axis=0)
    token_ref[...] = jnp.transpose(velocity)
    lane = lax.broadcasted_iota(jnp.int32, (32, HD), 1)
    by_px = [token_ref[pl.ds(px, 32, stride=4), :] for px in range(4)]
    for i in range(2):
        moved = jnp.zeros((32, HD), F32)
        for px in range(4):
            turn = (px - i) * 32 % HD
            piece = pltpu.roll(by_px[px], turn, axis=1) if turn else by_px[px]
            moved = jnp.where(lane // 32 == px, piece, moved)
        rows = slice(i * 32, i * 32 + 32)
        out_ref[rows, :] = (noisy_ref[rows, :].astype(F32) - moved).astype(BF16)
    out_ref[64:136, :] = prev_ref[...]


def clean_rows(parts, noisy, prev):
    part_specs = [
        pl.BlockSpec((HEADS // SPLIT, 72, HD), lambda i, part=part: (part, 0, 0))
        for part in range(SPLIT)
    ]
    return pl.pallas_call(
        clean_kernel,
        grid=(1,),
        in_specs=part_specs
        + [pl.BlockSpec((64, HD), lambda i: (0, 0)), pl.BlockSpec((72, HD), lambda i: (0, 0))],
        out_specs=pl.BlockSpec((136, HD), lambda i: (0, 0)),
        out_shape=jax.ShapeDtypeStruct((136, HD), BF16),
        scratch_shapes=[pltpu.VMEM((HD, HD), F32)],
        compiler_params=params(16),
        name="clean_rows",
    )(*(parts,) * SPLIT, noisy, prev)


def shift_rows(x, by):
    moved = pltpu.roll(x, by % 8, axis=1)
    y = lax.broadcasted_iota(jnp.int32, x.shape, 1)
    return jnp.where((y >= by) if by > 0 else (y < 8 + by), moved, 0.0)


def decode_kernel(
    mine_ref, in_ref, w_in_ref, b_in_ref, w_out_ref, b_out_ref,
    out_hbm, latent_ref, column_ref, part_ref, wide_ref, out_ref, out_sem,
):
    tiles = 8
    mine = mine_ref[0].astype(F32)
    flags = []
    for sender in range(4):
        new = in_ref[sender, 0:64, :].astype(F32)
        old = in_ref[sender, 64:136, :].astype(F32)
        owners = [old[64 + t : 65 + t] for t in range(4)]
        ranks = []
        for t in range(4):
            rank = jnp.zeros((1, HD), F32)
            for earlier in range(t):
                rank = rank + jnp.where(owners[earlier] == owners[t], 1.0, 0.0)
            ranks.append(rank)
        for slot in range(2):
            here = [
                jnp.where((owners[t] == mine) & (ranks[t] == slot), 1.0, 0.0) for t in range(4)
            ]
            flags.append(here[0] + here[1] + here[2] + here[3])
            masks = [jnp.broadcast_to(h, (8, HD)) > 0.5 for h in here]
            tile = sender * 2 + slot
            for frames, source in ((0, old), (1, new)):
                for i in range(2):
                    picked = jnp.zeros((8, HD), F32)
                    for t in range(4):
                        at = i * 32 + t * 8
                        picked = jnp.where(masks[t], source[at : at + 8], picked)
                    latent_ref[pl.ds(tile * 32 + frames * 16 + i, 8, stride=2), :] = picked
    latent = latent_ref[...].reshape(tiles * 4, 8, HD)
    by_row = [shift_rows(latent, 1), latent, shift_rows(latent, -1)]
    by_row = [x.reshape(tiles * 32, HD) for x in by_row]
    lane = lax.broadcasted_iota(jnp.int32, (tiles * 32, HD), 1)
    low = lane < 64
    for x in range(8):
        turn = (16 - 16 * x) % HD
        pair = [
            pltpu.roll(by_row[0], turn, axis=1) if turn else by_row[0],
            pltpu.roll(by_row[1], (turn + 64) % HD, axis=1) if turn != 64 else by_row[1],
            pltpu.roll(by_row[2], turn, axis=1) if turn else by_row[2],
        ]
        left = jnp.where(low, pair[0], pair[1])
        right = jnp.where(low, pair[2], 0.0)
        if x == 0:
            keep = (lane & 63) >= 16
            left, right = jnp.where(keep, left, 0.0), jnp.where(keep, right, 0.0)
        if x == 7:
            keep = (lane & 63) < 32
            left, right = jnp.where(keep, left, 0.0), jnp.where(keep, right, 0.0)
        taps = jnp.concatenate([left, right], axis=1).reshape(tiles, 4, 8, 2 * HD)
        columns = jnp.concatenate(
            [taps[:, dt : dt + 2].reshape(TOK, 2 * HD).astype(BF16) for dt in range(3)], axis=1
        )
        column_ref[x * TOK : (x + 1) * TOK, :] = columns
    mid = jnp.dot(column_ref[...], w_in_ref[...], preferred_element_type=F32) + b_in_ref[...]
    hidden = mid / (1.0 + jnp.exp(-mid))
    grouped = hidden.reshape(8 * TOK // 8, 8, 512)
    here = hidden.astype(BF16)
    bias = b_out_ref[...]
    for a in range(2):
        other = shift_rows(grouped, 1 if a == 0 else -1).reshape(8 * TOK, 512).astype(BF16)
        rows = jnp.concatenate([other, here] if a == 0 else [here, other], axis=1)
        part_ref[...] = jnp.dot(rows, w_out_ref[a], preferred_element_type=F32)
        for x in range(8):
            at = x * TOK
            first = part_ref[at : at + TOK, 128:256] + bias
            if x > 0:
                first = first + part_ref[at - TOK : at, 0:128]
            second = part_ref[at : at + TOK, 256:384] + bias
            if x < 7:
                second = second + part_ref[at + TOK : at + 2 * TOK, 384:512]
            wide_ref[pl.ds(a * 16 + 2 * x, TOK, stride=32), :] = first
            wide_ref[pl.ds(a * 16 + 2 * x + 1, TOK, stride=32), :] = second
    copies = []
    for tile in range(tiles):
        rows = slice(tile * 512, tile * 512 + 512)
        out_ref[rows, :] = jnp.where(flags[tile] > 0.5, wide_ref[rows, :], 0.0).astype(BF16)
        here = pl.ds(tile * 512, 512)
        copies.append(
            pltpu.make_async_copy(out_ref.at[here], out_hbm.at[here], out_sem.at[tile])
        )
        copies[tile].start()
    for copy in copies:
        copy.wait()


def decode(mine, arrived, w_in, b_in, w_out, b_out):
    vmem = pl.BlockSpec(memory_space=pltpu.VMEM)
    return pl.pallas_call(
        decode_kernel,
        in_specs=[pl.BlockSpec(memory_space=pltpu.SMEM)] + [vmem] * 5,
        out_specs=pl.BlockSpec(memory_space=pltpu.HBM),
        out_shape=jax.ShapeDtypeStruct((8 * 512, HD), BF16),
        scratch_shapes=[
            pltpu.VMEM((256, HD), F32),
            pltpu.VMEM((8 * TOK, 768), BF16),
            pltpu.VMEM((8 * TOK, 512), F32),
            pltpu.VMEM((8 * 512, HD), F32),
            pltpu.VMEM((8 * 512, HD), BF16),
            pltpu.SemaphoreType.DMA((8,)),
        ],
        compiler_params=pltpu.CompilerParams(vmem_limit_bytes=48 << 20),
        name="decode",
    )(mine, arrived, w_in, b_in, w_out, b_out)


def head_weight(velocity_weight):
    head = lax.axis_index("ctx")
    return lax.dynamic_slice_in_dim(velocity_weight, head * HD, HD, 0)


def place_in_weight(weight):
    split = weight.reshape(3, 3, 48, 512)
    return jnp.pad(split, ((0, 0), (0, 1), (0, 16), (0, 0))).reshape(3 * 4 * 64, 512)


def place_out_weight(weight):
    w = weight.reshape(3, 3, 512, 128).astype(F32)
    rows = [[w[0], w[1] + w[2]], [w[0] + w[1], w[2]]]
    phases = []
    for a in range(2):
        halves = []
        for r in rows[a]:
            halves.append(jnp.concatenate([r[0], r[1] + r[2], r[0] + r[1], r[2]], axis=1))
        phases.append(jnp.concatenate(halves, axis=0))
    return jnp.stack(phases).astype(BF16)


def latent_rows(latent):
    return latent.reshape(4, 2, 4, 2, HD).transpose(3, 0, 1, 2, 4).reshape(64, HD)


def exchange(x, axis):
    return lax.all_to_all(x, axis, split_axis=0, concat_axis=0, tiled=True)


def local(
    clip_queries,
    clip_keys,
    clip_values,
    cache_keys,
    cache_values,
    clip_pick,
    noisy_latent,
    prev_latent,
    velocity_weight,
    tile_owner,
    conv_in_weight,
    conv_in_bias,
    conv_out_weight,
    conv_out_bias,
):
    pick = clip_pick[0]
    current = (clip_queries[0], clip_keys[0], clip_values[0])
    clip = exchange(pack_first(pick, current, cache_keys[0], cache_values[0]), "ctx")
    window = pack_window(pick, cache_keys[0], cache_values[0])
    weight = head_weight(velocity_weight)
    w_in = place_in_weight(conv_in_weight)
    w_out = place_out_weight(conv_out_weight)
    noisy = latent_rows(noisy_latent[0])
    owners = jnp.broadcast_to(tile_owner[0].astype(BF16)[:, None], (4, HD))
    owners = jnp.pad(owners, ((0, 4), (0, 0)))
    prev = jnp.concatenate([latent_rows(prev_latent[0]), owners], axis=0)

    clip, window, weight, w_in, w_out, noisy, prev = lax.optimization_barrier(
        (clip, window, weight, w_in, w_out, noisy, prev)
    )
    window = exchange(window, "ctx")
    state = attend("first", clip, clip, 192)
    parts = attend("last", clip, window, TOK, state, weight)
    parts = exchange(parts, "ctx")
    arrived = lax.all_gather(clean_rows(parts, noisy, prev), "grp", axis=0)
    mine = lax.axis_index("grp").reshape(1)
    decoded = decode(
        mine, arrived, w_in, conv_in_bias.reshape(1, -1), w_out, conv_out_bias.reshape(1, -1)
    )
    return decoded.reshape(1, 1, 4, 2, 2, 256, 128)


def solution(mesh):
    in_specs = (
        P("grp", "ctx", None),
        P("grp", "ctx", None),
        P("grp", "ctx", None),
        P("grp", None, "ctx", None),
        P("grp", None, "ctx", None),
        P("grp", None),
        P("grp", "ctx", None, None),
        P("grp", "ctx", None, None),
        P(),
        P("grp", "ctx"),
        P(),
        P(),
        P(),
        P(),
    )
    out_specs = P("grp", "ctx", None, None, None, None, None)
    return jax.shard_map(local, mesh=mesh, in_specs=in_specs, out_specs=out_specs, check_vma=False)
```

```python
import math

import jax
import jax.numpy as jnp
from jax import lax
from jax.experimental import pallas as pl
from jax.experimental.pallas import tpu as pltpu
from jax.sharding import PartitionSpec as P

HEADS = 32
HD = 128
TOK = 128
F32 = jnp.float32
BF16 = jnp.bfloat16
SCALE = math.log2(math.e) / math.sqrt(HD)
HEADS_STEP = 8
BQ = 2048
LIMIT = 110.0
SPLIT = 4
KV_SPLIT = 1


def params(mib, axes=1):
    return pltpu.CompilerParams(
        vmem_limit_bytes=mib << 20, dimension_semantics=("arbitrary",) * axes
    )


def pack_first_kernel(pick_ref, q_ref, k_ref, v_ref, sink_k_ref, sink_v_ref, out_ref):
    for head in range(out_ref.shape[0]):
        lanes = slice(head * HD, (head + 1) * HD)
        out_ref[head, 0:TOK, :] = k_ref[:, lanes]
        out_ref[head, 192 : 192 + TOK, :] = v_ref[:, lanes]
        out_ref[head, 384 : 384 + TOK, :] = q_ref[:, lanes]
        for tile in range(4):
            rows = slice(tile * 32, tile * 32 + 16)
            at = TOK + tile * 16
            out_ref[head, at : at + 16, :] = sink_k_ref[0, rows, lanes]
            out_ref[head, 192 + at : 208 + at, :] = sink_v_ref[0, rows, lanes]


def pack_first(pick, current, keys, values):
    heads = 2 * HEADS_STEP
    own = pl.BlockSpec((TOK, heads * HD), lambda i, pick: (0, i))
    cached = pl.BlockSpec((1, TOK, heads * HD), lambda i, pick: (pick[0], 0, i))
    return pl.pallas_call(
        pack_first_kernel,
        grid_spec=pltpu.PrefetchScalarGridSpec(
            num_scalar_prefetch=1,
            grid=(HEADS // heads,),
            in_specs=[own] * 3 + [cached] * 2,
            out_specs=pl.BlockSpec((heads, 4 * TOK, HD), lambda i, pick: (i, 0, 0)),
        ),
        out_shape=jax.ShapeDtypeStruct((HEADS, 4 * TOK, HD), BF16),
        compiler_params=params(60),
        name="pack_first",
    )(pick, *current, keys, values)


def pack_window_kernel(pick_ref, k_ref, v_ref, out_ref):
    for head in range(HEADS_STEP):
        lanes = slice(head * HD, (head + 1) * HD)
        out_ref[head, 0:TOK, :] = k_ref[0, :, lanes]
        out_ref[head, TOK : 2 * TOK, :] = v_ref[0, :, lanes]


def pack_window(pick, keys, values):
    cached = pl.BlockSpec((1, TOK, HEADS_STEP * HD), lambda i, pick: (pick[1], 0, i))
    return pl.pallas_call(
        pack_window_kernel,
        grid_spec=pltpu.PrefetchScalarGridSpec(
            num_scalar_prefetch=1,
            grid=(HEADS // HEADS_STEP,),
            in_specs=[cached] * 2,
            out_specs=pl.BlockSpec((HEADS_STEP, 2 * TOK, HD), lambda i, pick: (i, 0, 0)),
        ),
        out_shape=jax.ShapeDtypeStruct((HEADS, 2 * TOK, HD), BF16),
        compiler_params=params(60),
        name="pack_window",
    )(pick, keys, values)


def key_blocks(refs, step):
    rows = refs[0].shape[1]
    return [
        ref[j : j + step].reshape(step * rows, HD)
        for ref in refs
        for j in range(0, ref.shape[0], step)
    ]


def score(k, q):
    return lax.dot_general(k, q, (((1,), (1,)), ((), ())), preferred_element_type=F32)


def mix(v, raised):
    return lax.dot_general(
        v, raised.astype(BF16), (((0,), (0,)), ((), ())), preferred_element_type=F32
    )


def fold_rows(x):
    return jnp.sum(x.reshape(x.shape[0] // 8, 8, x.shape[1]), axis=0)


def attend_bounded(q, k_refs, v_refs, step, totals, acc):
    keys, values = key_blocks(k_refs, step), key_blocks(v_refs, step)
    following = score(keys[0], q)
    for j in range(len(keys)):
        scores = following
        if j + 1 < len(keys):
            following = score(keys[j + 1], q)
        raised = jnp.exp2(scores * SCALE)
        mixed, total = mix(values[j], raised), fold_rows(raised)
        acc = mixed if acc is None else acc + mixed
        totals = total if totals is None else totals + total
    return totals, acc


def attend_any(q, k_refs, v_refs, step, top_ref, totals_ref, acc_ref):
    for k_ref, v_ref in zip(k_refs, v_refs):
        sources, rows = k_ref.shape[0], k_ref.shape[1]

        def body(j, carry, k_ref=k_ref, v_ref=v_ref, rows=rows):
            here = pl.ds(j * step, step)
            scores = score(k_ref[here].reshape(step * rows, HD), q)
            before = top_ref[0:1, :]
            top = jnp.maximum(before, jnp.max(scores, axis=0, keepdims=True))
            raised = jnp.exp2((scores - top) * SCALE)
            fade = jnp.exp2((before - top) * SCALE)
            mixed = mix(v_ref[here].reshape(step * rows, HD), raised)
            acc_ref[...] = acc_ref[...] * fade + mixed
            totals_ref[...] = totals_ref[...] * fade + fold_rows(raised)
            top_ref[...] = jnp.broadcast_to(top, top_ref.shape)
            return carry

        lax.fori_loop(0, sources // step, body, 0)


def bounded(q, k_refs):
    widest = [jnp.max(jnp.abs(k[...].reshape(-1, HD)), axis=0, keepdims=True) for k in k_refs]
    while len(widest) > 1:
        widest = [jnp.maximum(*widest[:2])] + widest[2:]
    widest = widest[0]
    reach = lax.dot_general(
        jnp.broadcast_to(widest, (16, HD)),
        jnp.abs(q),
        (((1,), (1,)), ((), ())),
        preferred_element_type=F32,
    )
    return jnp.max(reach) * (1.01 * SCALE) <= LIMIT


def attend_first_kernel(q_ref, *refs):
    k_refs, v_refs = refs[:KV_SPLIT], refs[KV_SPLIT : 2 * KV_SPLIT]
    slow_ref, top_ref, totals_ref, acc_ref = refs[2 * KV_SPLIT :]
    q = q_ref[...].reshape(BQ, HD)
    fits = bounded(q, k_refs)
    top_ref[...] = jnp.zeros(top_ref.shape, F32)
    totals_ref[...], acc_ref[...] = attend_bounded(q, k_refs, v_refs, 8, None, None)
    slow_ref[pl.program_id(0)] = jnp.where(fits, 0, 1)

    @pl.when(jnp.logical_not(fits))
    def _():
        top_ref[...] = jnp.full(top_ref.shape, -1e30, F32)
        totals_ref[...] = jnp.zeros(totals_ref.shape, F32)
        acc_ref[...] = jnp.zeros(acc_ref.shape, F32)
        attend_any(q, k_refs, v_refs, 4, top_ref, totals_ref, acc_ref)


def attend_last_kernel(q_ref, *refs):
    k_refs, v_refs = refs[:KV_SPLIT], refs[KV_SPLIT : 2 * KV_SPLIT]
    slow_ref, top_in_ref, totals_in_ref, acc_in_ref, weight_ref = refs[2 * KV_SPLIT : 2 * KV_SPLIT + 5]
    out_ref, top_ref, totals_ref, acc_ref = refs[2 * KV_SPLIT + 5 :]
    q = q_ref[...].reshape(BQ, HD)
    fits = bounded(q, k_refs) & (slow_ref[pl.program_id(0)] == 0)
    totals_ref[...], acc_ref[...] = attend_bounded(
        q, k_refs, v_refs, 8, totals_in_ref[...], acc_in_ref[...]
    )

    @pl.when(jnp.logical_not(fits))
    def _():
        top_ref[...] = top_in_ref[...]
        totals_ref[...] = totals_in_ref[...]
        acc_ref[...] = acc_in_ref[...]
        attend_any(q, k_refs, v_refs, 8, top_ref, totals_ref, acc_ref)

    totals = jnp.sum(totals_ref[...], axis=0, keepdims=True)
    attended = (acc_ref[...] / totals).astype(BF16)
    moved = lax.dot_general(
        weight_ref[...], attended, (((0,), (0,)), ((), ())), preferred_element_type=F32
    )
    wide = attended.astype(F32)
    squares = jnp.broadcast_to(jnp.sum(wide * wide, axis=0, keepdims=True), (8, BQ))
    block = jnp.concatenate([moved, squares], axis=0).astype(BF16)
    for dest in range(BQ // TOK):
        out_ref[dest] = block[:, dest * TOK : (dest + 1) * TOK]


def attend(kind, queries, keys_values, k_rows, state=(), weight=None):
    total = HEADS * TOK
    blocks = BQ // TOK
    steps = total // BQ
    q_spec = pl.BlockSpec((blocks, TOK, HD), lambda i: (i, 3, 0))
    kv_specs = [
        pl.BlockSpec((HEADS // KV_SPLIT, k_rows, HD), lambda i, part=part, place=place: (part, place, 0))
        for place in range(2)
        for part in range(KV_SPLIT)
    ]
    state_specs = [
        pl.BlockSpec(memory_space=pltpu.SMEM),
        pl.BlockSpec((8, BQ), lambda i: (0, i)),
        pl.BlockSpec((8, BQ), lambda i: (0, i)),
        pl.BlockSpec((HD, BQ), lambda i: (0, i)),
    ]
    state_shapes = [
        jax.ShapeDtypeStruct((steps,), jnp.int32),
        jax.ShapeDtypeStruct((8, total), F32),
        jax.ShapeDtypeStruct((8, total), F32),
        jax.ShapeDtypeStruct((HD, total), F32),
    ]
    in_specs = [q_spec] + kv_specs
    scratch = []
    args = (queries,) + (keys_values,) * (2 * KV_SPLIT)
    if kind == "first":
        body, out_specs, out_shape = attend_first_kernel, state_specs, state_shapes
    else:
        body = attend_last_kernel
        in_specs += state_specs + [pl.BlockSpec(weight.shape, lambda i: (0, 0))]
        args += (*state, weight)
        out_specs = pl.BlockSpec((blocks, 72, HD), lambda i: (i, 0, 0))
        out_shape = jax.ShapeDtypeStruct((HEADS, 72, HD), BF16)
        scratch = [
            pltpu.VMEM((8, BQ), F32),
            pltpu.VMEM((8, BQ), F32),
            pltpu.VMEM((HD, BQ), F32),
        ]
    keys = HEADS * k_rows
    return pl.pallas_call(
        body,
        grid=(steps,),
        in_specs=in_specs,
        out_specs=out_specs,
        out_shape=out_shape,
        scratch_shapes=scratch,
        compiler_params=params(60),
        cost_estimate=pl.CostEstimate(
            flops=6 * total * keys * HD,
            transcendentals=total * keys,
            bytes_accessed=8 << 20,
        ),
        name="attend_" + kind,
    )(*args)


def clean_kernel(*refs):
    parts, (noisy_ref, prev_ref, out_ref, token_ref) = refs[:SPLIT], refs[SPLIT:]
    width = HEADS * HD
    sums = [jnp.sum(part[...].astype(F32), axis=0) for part in parts]
    sums = (sums[0] + sums[1]) + (sums[2] + sums[3])
    scale = 1.0 / jnp.sqrt(sums[64:65] * (1.0 / width) + 1e-06)
    velocity = sums[0:64] * scale
    velocity = jnp.concatenate([velocity, jnp.zeros((64, HD), F32)], axis=0)
    token_ref[...] = jnp.transpose(velocity)
    lane = lax.broadcasted_iota(jnp.int32, (32, HD), 1)
    by_px = [token_ref[pl.ds(px, 32, stride=4), :] for px in range(4)]
    for i in range(2):
        moved = jnp.zeros((32, HD), F32)
        for px in range(4):
            turn = (px - i) * 32 % HD
            piece = pltpu.roll(by_px[px], turn, axis=1) if turn else by_px[px]
            moved = jnp.where(lane // 32 == px, piece, moved)
        rows = slice(i * 32, i * 32 + 32)
        out_ref[rows, :] = (noisy_ref[rows, :].astype(F32) - moved).astype(BF16)
    out_ref[64:136, :] = prev_ref[...]


def clean_rows(parts, noisy, prev):
    part_specs = [
        pl.BlockSpec((HEADS // SPLIT, 72, HD), lambda i, part=part: (part, 0, 0))
        for part in range(SPLIT)
    ]
    return pl.pallas_call(
        clean_kernel,
        grid=(1,),
        in_specs=part_specs
        + [pl.BlockSpec((64, HD), lambda i: (0, 0)), pl.BlockSpec((72, HD), lambda i: (0, 0))],
        out_specs=pl.BlockSpec((136, HD), lambda i: (0, 0)),
        out_shape=jax.ShapeDtypeStruct((136, HD), BF16),
        scratch_shapes=[pltpu.VMEM((HD, HD), F32)],
        compiler_params=params(16),
        name="clean_rows",
    )(*(parts,) * SPLIT, noisy, prev)


def shift_rows(x, by):
    moved = pltpu.roll(x, by % 8, axis=1)
    y = lax.broadcasted_iota(jnp.int32, x.shape, 1)
    return jnp.where((y >= by) if by > 0 else (y < 8 + by), moved, 0.0)


def decode_kernel(
    mine_ref, in_ref, w_in_ref, b_in_ref, w_out_ref, b_out_ref,
    out_hbm, latent_ref, column_ref, part_ref, wide_ref, out_ref, out_sem,
):
    tiles = 8
    mine = mine_ref[0].astype(F32)
    flags = []
    for sender in range(4):
        new = in_ref[sender, 0:64, :].astype(F32)
        old = in_ref[sender, 64:136, :].astype(F32)
        owners = [old[64 + t : 65 + t] for t in range(4)]
        ranks = []
        for t in range(4):
            rank = jnp.zeros((1, HD), F32)
            for earlier in range(t):
                rank = rank + jnp.where(owners[earlier] == owners[t], 1.0, 0.0)
            ranks.append(rank)
        for slot in range(2):
            here = [
                jnp.where((owners[t] == mine) & (ranks[t] == slot), 1.0, 0.0) for t in range(4)
            ]
            flags.append(here[0] + here[1] + here[2] + here[3])
            masks = [jnp.broadcast_to(h, (8, HD)) > 0.5 for h in here]
            tile = sender * 2 + slot
            for frames, source in ((0, old), (1, new)):
                for i in range(2):
                    picked = jnp.zeros((8, HD), F32)
                    for t in range(4):
                        at = i * 32 + t * 8
                        picked = jnp.where(masks[t], source[at : at + 8], picked)
                    latent_ref[pl.ds(tile * 32 + frames * 16 + i, 8, stride=2), :] = picked
    latent = latent_ref[...].reshape(tiles * 4, 8, HD)
    by_row = [shift_rows(latent, 1), latent, shift_rows(latent, -1)]
    by_row = [x.reshape(tiles * 32, HD) for x in by_row]
    lane = lax.broadcasted_iota(jnp.int32, (tiles * 32, HD), 1)
    low = lane < 64
    for x in range(8):
        turn = (16 - 16 * x) % HD
        pair = [
            pltpu.roll(by_row[0], turn, axis=1) if turn else by_row[0],
            pltpu.roll(by_row[1], (turn + 64) % HD, axis=1) if turn != 64 else by_row[1],
            pltpu.roll(by_row[2], turn, axis=1) if turn else by_row[2],
        ]
        left = jnp.where(low, pair[0], pair[1])
        right = jnp.where(low, pair[2], 0.0)
        if x == 0:
            keep = (lane & 63) >= 16
            left, right = jnp.where(keep, left, 0.0), jnp.where(keep, right, 0.0)
        if x == 7:
            keep = (lane & 63) < 32
            left, right = jnp.where(keep, left, 0.0), jnp.where(keep, right, 0.0)
        taps = jnp.concatenate([left, right], axis=1).reshape(tiles, 4, 8, 2 * HD)
        columns = jnp.concatenate(
            [taps[:, dt : dt + 2].reshape(TOK, 2 * HD).astype(BF16) for dt in range(3)], axis=1
        )
        column_ref[x * TOK : (x + 1) * TOK, :] = columns
    mid = jnp.dot(column_ref[...], w_in_ref[...], preferred_element_type=F32) + b_in_ref[...]
    hidden = mid / (1.0 + jnp.exp(-mid))
    grouped = hidden.reshape(8 * TOK // 8, 8, 512)
    here = hidden.astype(BF16)
    bias = b_out_ref[...]
    for a in range(2):
        other = shift_rows(grouped, 1 if a == 0 else -1).reshape(8 * TOK, 512).astype(BF16)
        rows = jnp.concatenate([other, here] if a == 0 else [here, other], axis=1)
        part_ref[...] = jnp.dot(rows, w_out_ref[a], preferred_element_type=F32)
        for x in range(8):
            at = x * TOK
            first = part_ref[at : at + TOK, 128:256] + bias
            if x > 0:
                first = first + part_ref[at - TOK : at, 0:128]
            second = part_ref[at : at + TOK, 256:384] + bias
            if x < 7:
                second = second + part_ref[at + TOK : at + 2 * TOK, 384:512]
            wide_ref[pl.ds(a * 16 + 2 * x, TOK, stride=32), :] = first
            wide_ref[pl.ds(a * 16 + 2 * x + 1, TOK, stride=32), :] = second
    copies = []
    for tile in range(tiles):
        rows = slice(tile * 512, tile * 512 + 512)
        out_ref[rows, :] = jnp.where(flags[tile] > 0.5, wide_ref[rows, :], 0.0).astype(BF16)
        here = pl.ds(tile * 512, 512)
        copies.append(
            pltpu.make_async_copy(out_ref.at[here], out_hbm.at[here], out_sem.at[tile])
        )
        copies[tile].start()
    for copy in copies:
        copy.wait()


def decode(mine, arrived, w_in, b_in, w_out, b_out):
    vmem = pl.BlockSpec(memory_space=pltpu.VMEM)
    return pl.pallas_call(
        decode_kernel,
        in_specs=[pl.BlockSpec(memory_space=pltpu.SMEM)] + [vmem] * 5,
        out_specs=pl.BlockSpec(memory_space=pltpu.HBM),
        out_shape=jax.ShapeDtypeStruct((8 * 512, HD), BF16),
        scratch_shapes=[
            pltpu.VMEM((256, HD), F32),
            pltpu.VMEM((8 * TOK, 768), BF16),
            pltpu.VMEM((8 * TOK, 512), F32),
            pltpu.VMEM((8 * 512, HD), F32),
            pltpu.VMEM((8 * 512, HD), BF16),
            pltpu.SemaphoreType.DMA((8,)),
        ],
        compiler_params=pltpu.CompilerParams(vmem_limit_bytes=48 << 20),
        name="decode",
    )(mine, arrived, w_in, b_in, w_out, b_out)


def head_weight(velocity_weight):
    head = lax.axis_index("ctx")
    return lax.dynamic_slice_in_dim(velocity_weight, head * HD, HD, 0)


def place_in_weight(weight):
    split = weight.reshape(3, 3, 48, 512)
    return jnp.pad(split, ((0, 0), (0, 1), (0, 16), (0, 0))).reshape(3 * 4 * 64, 512)


def place_out_weight(weight):
    w = weight.reshape(3, 3, 512, 128).astype(F32)
    rows = [[w[0], w[1] + w[2]], [w[0] + w[1], w[2]]]
    phases = []
    for a in range(2):
        halves = []
        for r in rows[a]:
            halves.append(jnp.concatenate([r[0], r[1] + r[2], r[0] + r[1], r[2]], axis=1))
        phases.append(jnp.concatenate(halves, axis=0))
    return jnp.stack(phases).astype(BF16)


def latent_rows(latent):
    return latent.reshape(4, 2, 4, 2, HD).transpose(3, 0, 1, 2, 4).reshape(64, HD)


def exchange(x, axis):
    return lax.all_to_all(x, axis, split_axis=0, concat_axis=0, tiled=True)


def local(
    clip_queries,
    clip_keys,
    clip_values,
    cache_keys,
    cache_values,
    clip_pick,
    noisy_latent,
    prev_latent,
    velocity_weight,
    tile_owner,
    conv_in_weight,
    conv_in_bias,
    conv_out_weight,
    conv_out_bias,
):
    pick = clip_pick[0]
    current = (clip_queries[0], clip_keys[0], clip_values[0])
    clip = exchange(pack_first(pick, current, cache_keys[0], cache_values[0]), "ctx")
    window = pack_window(pick, cache_keys[0], cache_values[0])
    weight = head_weight(velocity_weight)
    w_in = place_in_weight(conv_in_weight)
    w_out = place_out_weight(conv_out_weight)
    noisy = latent_rows(noisy_latent[0])
    owners = jnp.broadcast_to(tile_owner[0].astype(BF16)[:, None], (4, HD))
    owners = jnp.pad(owners, ((0, 4), (0, 0)))
    prev = jnp.concatenate([latent_rows(prev_latent[0]), owners], axis=0)

    clip, window, weight, w_in, w_out, noisy, prev = lax.optimization_barrier(
        (clip, window, weight, w_in, w_out, noisy, prev)
    )
    window = exchange(window, "ctx")
    state = attend("first", clip, clip, 192)
    parts = attend("last", clip, window, TOK, state, weight)
    parts = exchange(parts, "ctx")
    arrived = lax.all_gather(clean_rows(parts, noisy, prev), "grp", axis=0)
    mine = lax.axis_index("grp").reshape(1)
    decoded = decode(
        mine, arrived, w_in, conv_in_bias.reshape(1, -1), w_out, conv_out_bias.reshape(1, -1)
    )
    return decoded.reshape(1, 1, 4, 2, 2, 256, 128)


def solution(mesh):
    in_specs = (
        P("grp", "ctx", None),
        P("grp", "ctx", None),
        P("grp", "ctx", None),
        P("grp", None, "ctx", None),
        P("grp", None, "ctx", None),
        P("grp", None),
        P("grp", "ctx", None, None),
        P("grp", "ctx", None, None),
        P(),
        P("grp", "ctx"),
        P(),
        P(),
        P(),
        P(),
    )
    out_specs = P("grp", "ctx", None, None, None, None, None)
    return jax.shard_map(local, mesh=mesh, in_specs=in_specs, out_specs=out_specs, check_vma=False)
```

```python
import math

import jax
import jax.numpy as jnp
from jax import lax
from jax.experimental import pallas as pl
from jax.experimental.pallas import tpu as pltpu
from jax.sharding import PartitionSpec as P

HEADS = 32
HD = 128
TOK = 128
F32 = jnp.float32
BF16 = jnp.bfloat16
SCALE = math.log2(math.e) / math.sqrt(HD)
HEADS_STEP = 8
BQ = 2048
LIMIT = 110.0
SPLIT = 4
KV_SPLIT = 1


def params(mib, axes=1):
    return pltpu.CompilerParams(
        vmem_limit_bytes=mib << 20, dimension_semantics=("arbitrary",) * axes
    )


def pack_first_kernel(
    pick_ref, q_ref, k_ref, v_ref, sink_k_ref, sink_v_ref, out_hbm, out_ref, out_sem
):
    steps, heads = out_ref.shape[0], out_ref.shape[1]
    part = heads // SPLIT
    here = pl.program_id(0)

    def store(step, n):
        return pltpu.make_async_copy(
            out_ref.at[step, pl.ds(n * part, part)],
            out_hbm.at[pl.ds(step * heads + n * part, part)],
            out_sem.at[step, n],
        )

    for head in range(heads):
        lanes = slice(head * HD, (head + 1) * HD)
        out_ref[here, head, 0:TOK, :] = k_ref[:, lanes]
        out_ref[here, head, 192 : 192 + TOK, :] = v_ref[:, lanes]
        out_ref[here, head, 384 : 384 + TOK, :] = q_ref[:, lanes]
        for tile in range(4):
            at = TOK + tile * 16
            out_ref[here, head, at : at + 16, :] = sink_k_ref[0, tile, 0, :, lanes]
            out_ref[here, head, 192 + at : 208 + at, :] = sink_v_ref[0, tile, 0, :, lanes]
        if head % part == part - 1:
            store(here, head // part).start()

    @pl.when(here == steps - 1)
    def _():
        for step in range(steps):
            for n in range(SPLIT):
                store(step, n).wait()


def pack_first(pick, current, keys, values):
    heads = 2 * HEADS_STEP
    steps = HEADS // heads
    own = pl.BlockSpec((TOK, heads * HD), lambda i, pick: (0, i))
    cached = pl.BlockSpec((1, 4, 1, 16, heads * HD), lambda i, pick: (pick[0], 0, 0, 0, i))
    by_frame = [x.reshape(x.shape[0], 4, 2, 16, x.shape[2]) for x in (keys, values)]
    return pl.pallas_call(
        pack_first_kernel,
        grid_spec=pltpu.PrefetchScalarGridSpec(
            num_scalar_prefetch=1,
            grid=(steps,),
            in_specs=[own] * 3 + [cached] * 2,
            out_specs=pl.BlockSpec(memory_space=pltpu.HBM),
            scratch_shapes=[
                pltpu.VMEM((steps, heads, 4 * TOK, HD), BF16),
                pltpu.SemaphoreType.DMA((steps, SPLIT)),
            ],
        ),
        out_shape=jax.ShapeDtypeStruct((HEADS, 4 * TOK, HD), BF16),
        compiler_params=params(60),
        name="pack_first",
    )(pick, *current, *by_frame)


def pack_window_kernel(pick_ref, k_ref, v_ref, out_ref):
    for head in range(HEADS_STEP):
        lanes = slice(head * HD, (head + 1) * HD)
        out_ref[head, 0:TOK, :] = k_ref[0, :, lanes]
        out_ref[head, TOK : 2 * TOK, :] = v_ref[0, :, lanes]


def pack_window(pick, keys, values):
    cached = pl.BlockSpec((1, TOK, HEADS_STEP * HD), lambda i, pick: (pick[1], 0, i))
    return pl.pallas_call(
        pack_window_kernel,
        grid_spec=pltpu.PrefetchScalarGridSpec(
            num_scalar_prefetch=1,
            grid=(HEADS // HEADS_STEP,),
            in_specs=[cached] * 2,
            out_specs=pl.BlockSpec((HEADS_STEP, 2 * TOK, HD), lambda i, pick: (i, 0, 0)),
        ),
        out_shape=jax.ShapeDtypeStruct((HEADS, 2 * TOK, HD), BF16),
        compiler_params=params(60),
        name="pack_window",
    )(pick, keys, values)


def key_blocks(refs, step):
    rows = refs[0].shape[1]
    return [
        ref[j : j + step].reshape(step * rows, HD)
        for ref in refs
        for j in range(0, ref.shape[0], step)
    ]


def score(k, q):
    return lax.dot_general(k, q, (((1,), (1,)), ((), ())), preferred_element_type=F32)


def mix(v, raised):
    return lax.dot_general(
        v, raised.astype(BF16), (((0,), (0,)), ((), ())), preferred_element_type=F32
    )


def fold_rows(x):
    return jnp.sum(x.reshape(x.shape[0] // 8, 8, x.shape[1]), axis=0)


def attend_bounded(q, k_refs, v_refs, step, totals, acc):
    keys, values = key_blocks(k_refs, step), key_blocks(v_refs, step)
    following = score(keys[0], q)
    for j in range(len(keys)):
        scores = following
        if j + 1 < len(keys):
            following = score(keys[j + 1], q)
        raised = jnp.exp2(scores * SCALE)
        mixed, total = mix(values[j], raised), fold_rows(raised)
        acc = mixed if acc is None else acc + mixed
        totals = total if totals is None else totals + total
    return totals, acc


def attend_any(q, k_refs, v_refs, step, top_ref, totals_ref, acc_ref):
    for k_ref, v_ref in zip(k_refs, v_refs):
        sources, rows = k_ref.shape[0], k_ref.shape[1]

        def body(j, carry, k_ref=k_ref, v_ref=v_ref, rows=rows):
            here = pl.ds(j * step, step)
            scores = score(k_ref[here].reshape(step * rows, HD), q)
            before = top_ref[0:1, :]
            top = jnp.maximum(before, jnp.max(scores, axis=0, keepdims=True))
            raised = jnp.exp2((scores - top) * SCALE)
            fade = jnp.exp2((before - top) * SCALE)
            mixed = mix(v_ref[here].reshape(step * rows, HD), raised)
            acc_ref[...] = acc_ref[...] * fade + mixed
            totals_ref[...] = totals_ref[...] * fade + fold_rows(raised)
            top_ref[...] = jnp.broadcast_to(top, top_ref.shape)
            return carry

        lax.fori_loop(0, sources // step, body, 0)


def bounded(q, k_refs):
    widest = [jnp.max(jnp.abs(k[...].reshape(-1, HD)), axis=0, keepdims=True) for k in k_refs]
    while len(widest) > 1:
        widest = [jnp.maximum(*widest[:2])] + widest[2:]
    widest = widest[0]
    reach = lax.dot_general(
        jnp.broadcast_to(widest, (16, HD)),
        jnp.abs(q),
        (((1,), (1,)), ((), ())),
        preferred_element_type=F32,
    )
    return jnp.max(reach) * (1.01 * SCALE) <= LIMIT


def attend_first_kernel(q_ref, *refs):
    k_refs, v_refs = refs[:KV_SPLIT], refs[KV_SPLIT : 2 * KV_SPLIT]
    slow_ref, top_ref, totals_ref, acc_ref = refs[2 * KV_SPLIT :]
    q = q_ref[...].reshape(BQ, HD)
    fits = bounded(q, k_refs)
    top_ref[...] = jnp.zeros(top_ref.shape, F32)
    totals_ref[...], acc_ref[...] = attend_bounded(q, k_refs, v_refs, 8, None, None)
    slow_ref[pl.program_id(0)] = jnp.where(fits, 0, 1)

    @pl.when(jnp.logical_not(fits))
    def _():
        top_ref[...] = jnp.full(top_ref.shape, -1e30, F32)
        totals_ref[...] = jnp.zeros(totals_ref.shape, F32)
        acc_ref[...] = jnp.zeros(acc_ref.shape, F32)
        attend_any(q, k_refs, v_refs, 4, top_ref, totals_ref, acc_ref)


def attend_last_kernel(q_ref, *refs):
    k_refs, v_refs = refs[:KV_SPLIT], refs[KV_SPLIT : 2 * KV_SPLIT]
    slow_ref, top_in_ref, totals_in_ref, acc_in_ref, weight_ref = refs[2 * KV_SPLIT : 2 * KV_SPLIT + 5]
    out_ref, top_ref, totals_ref, acc_ref = refs[2 * KV_SPLIT + 5 :]
    q = q_ref[...].reshape(BQ, HD)
    fits = bounded(q, k_refs) & (slow_ref[pl.program_id(0)] == 0)
    totals_ref[...], acc_ref[...] = attend_bounded(
        q, k_refs, v_refs, 8, totals_in_ref[...], acc_in_ref[...]
    )

    @pl.when(jnp.logical_not(fits))
    def _():
        top_ref[...] = top_in_ref[...]
        totals_ref[...] = totals_in_ref[...]
        acc_ref[...] = acc_in_ref[...]
        attend_any(q, k_refs, v_refs, 8, top_ref, totals_ref, acc_ref)

    totals = jnp.sum(totals_ref[...], axis=0, keepdims=True)
    attended = (acc_ref[...] / totals).astype(BF16)
    moved = lax.dot_general(
        weight_ref[...], attended, (((0,), (0,)), ((), ())), preferred_element_type=F32
    )
    wide = attended.astype(F32)
    squares = jnp.broadcast_to(jnp.sum(wide * wide, axis=0, keepdims=True), (8, BQ))
    block = jnp.concatenate([moved, squares], axis=0).astype(BF16)
    for dest in range(BQ // TOK):
        out_ref[dest] = block[:, dest * TOK : (dest + 1) * TOK]


def attend(kind, queries, keys_values, k_rows, state=(), weight=None):
    total = HEADS * TOK
    blocks = BQ // TOK
    steps = total // BQ
    q_spec = pl.BlockSpec((blocks, TOK, HD), lambda i: (i, 3, 0))
    kv_specs = [
        pl.BlockSpec((HEADS // KV_SPLIT, k_rows, HD), lambda i, part=part, place=place: (part, place, 0))
        for place in range(2)
        for part in range(KV_SPLIT)
    ]
    state_specs = [
        pl.BlockSpec(memory_space=pltpu.SMEM),
        pl.BlockSpec((8, BQ), lambda i: (0, i)),
        pl.BlockSpec((8, BQ), lambda i: (0, i)),
        pl.BlockSpec((HD, BQ), lambda i: (0, i)),
    ]
    state_shapes = [
        jax.ShapeDtypeStruct((steps,), jnp.int32),
        jax.ShapeDtypeStruct((8, total), F32),
        jax.ShapeDtypeStruct((8, total), F32),
        jax.ShapeDtypeStruct((HD, total), F32),
    ]
    in_specs = [q_spec] + kv_specs
    scratch = []
    args = (queries,) + (keys_values,) * (2 * KV_SPLIT)
    if kind == "first":
        body, out_specs, out_shape = attend_first_kernel, state_specs, state_shapes
    else:
        body = attend_last_kernel
        in_specs += state_specs + [pl.BlockSpec(weight.shape, lambda i: (0, 0))]
        args += (*state, weight)
        out_specs = pl.BlockSpec((blocks, 72, HD), lambda i: (i, 0, 0))
        out_shape = jax.ShapeDtypeStruct((HEADS, 72, HD), BF16)
        scratch = [
            pltpu.VMEM((8, BQ), F32),
            pltpu.VMEM((8, BQ), F32),
            pltpu.VMEM((HD, BQ), F32),
        ]
    keys = HEADS * k_rows
    return pl.pallas_call(
        body,
        grid=(steps,),
        in_specs=in_specs,
        out_specs=out_specs,
        out_shape=out_shape,
        scratch_shapes=scratch,
        compiler_params=params(60),
        cost_estimate=pl.CostEstimate(
            flops=6 * total * keys * HD,
            transcendentals=total * keys,
            bytes_accessed=8 << 20,
        ),
        name="attend_" + kind,
    )(*args)


def clean_kernel(*refs):
    parts, (noisy_ref, prev_ref, out_ref, token_ref) = refs[:SPLIT], refs[SPLIT:]
    width = HEADS * HD
    sums = [jnp.sum(part[...].astype(F32), axis=0) for part in parts]
    sums = (sums[0] + sums[1]) + (sums[2] + sums[3])
    scale = 1.0 / jnp.sqrt(sums[64:65] * (1.0 / width) + 1e-06)
    velocity = sums[0:64] * scale
    velocity = jnp.concatenate([velocity, jnp.zeros((64, HD), F32)], axis=0)
    token_ref[...] = jnp.transpose(velocity)
    lane = lax.broadcasted_iota(jnp.int32, (32, HD), 1)
    by_px = [token_ref[pl.ds(px, 32, stride=4), :] for px in range(4)]
    for i in range(2):
        moved = jnp.zeros((32, HD), F32)
        for px in range(4):
            turn = (px - i) * 32 % HD
            piece = pltpu.roll(by_px[px], turn, axis=1) if turn else by_px[px]
            moved = jnp.where(lane // 32 == px, piece, moved)
        rows = slice(i * 32, i * 32 + 32)
        out_ref[rows, :] = (noisy_ref[rows, :].astype(F32) - moved).astype(BF16)
    out_ref[64:136, :] = prev_ref[...]


def clean_rows(parts, noisy, prev):
    part_specs = [
        pl.BlockSpec((HEADS // SPLIT, 72, HD), lambda i, part=part: (part, 0, 0))
        for part in range(SPLIT)
    ]
    return pl.pallas_call(
        clean_kernel,
        grid=(1,),
        in_specs=part_specs
        + [pl.BlockSpec((64, HD), lambda i: (0, 0)), pl.BlockSpec((72, HD), lambda i: (0, 0))],
        out_specs=pl.BlockSpec((136, HD), lambda i: (0, 0)),
        out_shape=jax.ShapeDtypeStruct((136, HD), BF16),
        scratch_shapes=[pltpu.VMEM((HD, HD), F32)],
        compiler_params=params(16),
        name="clean_rows",
    )(*(parts,) * SPLIT, noisy, prev)


def shift_rows(x, by):
    moved = pltpu.roll(x, by % 8, axis=1)
    y = lax.broadcasted_iota(jnp.int32, x.shape, 1)
    return jnp.where((y >= by) if by > 0 else (y < 8 + by), moved, 0.0)


def decode_kernel(
    mine_ref, in_ref, w_in_ref, b_in_ref, w_out_ref, b_out_ref,
    out_hbm, latent_ref, column_ref, part_ref, wide_ref, out_ref, out_sem,
):
    tiles = 8
    mine = mine_ref[0].astype(F32)
    flags = []
    for sender in range(4):
        new = in_ref[sender, 0:64, :].astype(F32)
        old = in_ref[sender, 64:136, :].astype(F32)
        owners = [old[64 + t : 65 + t] for t in range(4)]
        ranks = []
        for t in range(4):
            rank = jnp.zeros((1, HD), F32)
            for earlier in range(t):
                rank = rank + jnp.where(owners[earlier] == owners[t], 1.0, 0.0)
            ranks.append(rank)
        for slot in range(2):
            here = [
                jnp.where((owners[t] == mine) & (ranks[t] == slot), 1.0, 0.0) for t in range(4)
            ]
            flags.append(here[0] + here[1] + here[2] + here[3])
            masks = [jnp.broadcast_to(h, (8, HD)) > 0.5 for h in here]
            tile = sender * 2 + slot
            for frames, source in ((0, old), (1, new)):
                for i in range(2):
                    picked = jnp.zeros((8, HD), F32)
                    for t in range(4):
                        at = i * 32 + t * 8
                        picked = jnp.where(masks[t], source[at : at + 8], picked)
                    latent_ref[pl.ds(tile * 32 + frames * 16 + i, 8, stride=2), :] = picked
    latent = latent_ref[...].reshape(tiles * 4, 8, HD)
    by_row = [shift_rows(latent, 1), latent, shift_rows(latent, -1)]
    by_row = [x.reshape(tiles * 32, HD) for x in by_row]
    lane = lax.broadcasted_iota(jnp.int32, (tiles * 32, HD), 1)
    low = lane < 64
    for x in range(8):
        turn = (16 - 16 * x) % HD
        pair = [
            pltpu.roll(by_row[0], turn, axis=1) if turn else by_row[0],
            pltpu.roll(by_row[1], (turn + 64) % HD, axis=1) if turn != 64 else by_row[1],
            pltpu.roll(by_row[2], turn, axis=1) if turn else by_row[2],
        ]
        left = jnp.where(low, pair[0], pair[1])
        right = jnp.where(low, pair[2], 0.0)
        if x == 0:
            keep = (lane & 63) >= 16
            left, right = jnp.where(keep, left, 0.0), jnp.where(keep, right, 0.0)
        if x == 7:
            keep = (lane & 63) < 32
            left, right = jnp.where(keep, left, 0.0), jnp.where(keep, right, 0.0)
        taps = jnp.concatenate([left, right], axis=1).reshape(tiles, 4, 8, 2 * HD)
        columns = jnp.concatenate(
            [taps[:, dt : dt + 2].reshape(TOK, 2 * HD).astype(BF16) for dt in range(3)], axis=1
        )
        column_ref[x * TOK : (x + 1) * TOK, :] = columns
    mid = jnp.dot(column_ref[...], w_in_ref[...], preferred_element_type=F32) + b_in_ref[...]
    hidden = mid / (1.0 + jnp.exp(-mid))
    grouped = hidden.reshape(8 * TOK // 8, 8, 512)
    here = hidden.astype(BF16)
    bias = b_out_ref[...]
    for a in range(2):
        other = shift_rows(grouped, 1 if a == 0 else -1).reshape(8 * TOK, 512).astype(BF16)
        rows = jnp.concatenate([other, here] if a == 0 else [here, other], axis=1)
        part_ref[...] = jnp.dot(rows, w_out_ref[a], preferred_element_type=F32)
        for x in range(8):
            at = x * TOK
            first = part_ref[at : at + TOK, 128:256] + bias
            if x > 0:
                first = first + part_ref[at - TOK : at, 0:128]
            second = part_ref[at : at + TOK, 256:384] + bias
            if x < 7:
                second = second + part_ref[at + TOK : at + 2 * TOK, 384:512]
            wide_ref[pl.ds(a * 16 + 2 * x, TOK, stride=32), :] = first
            wide_ref[pl.ds(a * 16 + 2 * x + 1, TOK, stride=32), :] = second
    copies = []
    for tile in range(tiles):
        rows = slice(tile * 512, tile * 512 + 512)
        out_ref[rows, :] = jnp.where(flags[tile] > 0.5, wide_ref[rows, :], 0.0).astype(BF16)
        here = pl.ds(tile * 512, 512)
        copies.append(
            pltpu.make_async_copy(out_ref.at[here], out_hbm.at[here], out_sem.at[tile])
        )
        copies[tile].start()
    for copy in copies:
        copy.wait()


def decode(mine, arrived, w_in, b_in, w_out, b_out):
    vmem = pl.BlockSpec(memory_space=pltpu.VMEM)
    return pl.pallas_call(
        decode_kernel,
        in_specs=[pl.BlockSpec(memory_space=pltpu.SMEM)] + [vmem] * 5,
        out_specs=pl.BlockSpec(memory_space=pltpu.HBM),
        out_shape=jax.ShapeDtypeStruct((8 * 512, HD), BF16),
        scratch_shapes=[
            pltpu.VMEM((256, HD), F32),
            pltpu.VMEM((8 * TOK, 768), BF16),
            pltpu.VMEM((8 * TOK, 512), F32),
            pltpu.VMEM((8 * 512, HD), F32),
            pltpu.VMEM((8 * 512, HD), BF16),
            pltpu.SemaphoreType.DMA((8,)),
        ],
        compiler_params=pltpu.CompilerParams(vmem_limit_bytes=48 << 20),
        name="decode",
    )(mine, arrived, w_in, b_in, w_out, b_out)


def head_weight(velocity_weight):
    head = lax.axis_index("ctx")
    return lax.dynamic_slice_in_dim(velocity_weight, head * HD, HD, 0)


def place_in_weight(weight):
    split = weight.reshape(3, 3, 48, 512)
    return jnp.pad(split, ((0, 0), (0, 1), (0, 16), (0, 0))).reshape(3 * 4 * 64, 512)


def place_out_weight(weight):
    w = weight.reshape(3, 3, 512, 128).astype(F32)
    rows = [[w[0], w[1] + w[2]], [w[0] + w[1], w[2]]]
    phases = []
    for a in range(2):
        halves = []
        for r in rows[a]:
            halves.append(jnp.concatenate([r[0], r[1] + r[2], r[0] + r[1], r[2]], axis=1))
        phases.append(jnp.concatenate(halves, axis=0))
    return jnp.stack(phases).astype(BF16)


def latent_rows(latent):
    return latent.reshape(4, 2, 4, 2, HD).transpose(3, 0, 1, 2, 4).reshape(64, HD)


def exchange(x, axis):
    return lax.all_to_all(x, axis, split_axis=0, concat_axis=0, tiled=True)


def local(
    clip_queries,
    clip_keys,
    clip_values,
    cache_keys,
    cache_values,
    clip_pick,
    noisy_latent,
    prev_latent,
    velocity_weight,
    tile_owner,
    conv_in_weight,
    conv_in_bias,
    conv_out_weight,
    conv_out_bias,
):
    pick = clip_pick[0]
    current = (clip_queries[0], clip_keys[0], clip_values[0])
    clip = exchange(pack_first(pick, current, cache_keys[0], cache_values[0]), "ctx")
    window = pack_window(pick, cache_keys[0], cache_values[0])
    weight = head_weight(velocity_weight)
    w_in = place_in_weight(conv_in_weight)
    w_out = place_out_weight(conv_out_weight)
    noisy = latent_rows(noisy_latent[0])
    owners = jnp.broadcast_to(tile_owner[0].astype(BF16)[:, None], (4, HD))
    owners = jnp.pad(owners, ((0, 4), (0, 0)))
    prev = jnp.concatenate([latent_rows(prev_latent[0]), owners], axis=0)

    clip, window, weight, w_in, w_out, noisy, prev = lax.optimization_barrier(
        (clip, window, weight, w_in, w_out, noisy, prev)
    )
    window = exchange(window, "ctx")
    state = attend("first", clip, clip, 192)
    parts = attend("last", clip, window, TOK, state, weight)
    parts = exchange(parts, "ctx")
    arrived = lax.all_gather(clean_rows(parts, noisy, prev), "grp", axis=0)
    mine = lax.axis_index("grp").reshape(1)
    decoded = decode(
        mine, arrived, w_in, conv_in_bias.reshape(1, -1), w_out, conv_out_bias.reshape(1, -1)
    )
    return decoded.reshape(1, 1, 4, 2, 2, 256, 128)


def solution(mesh):
    in_specs = (
        P("grp", "ctx", None),
        P("grp", "ctx", None),
        P("grp", "ctx", None),
        P("grp", None, "ctx", None),
        P("grp", None, "ctx", None),
        P("grp", None),
        P("grp", "ctx", None, None),
        P("grp", "ctx", None, None),
        P(),
        P("grp", "ctx"),
        P(),
        P(),
        P(),
        P(),
    )
    out_specs = P("grp", "ctx", None, None, None, None, None)
    return jax.shard_map(local, mesh=mesh, in_specs=in_specs, out_specs=out_specs, check_vma=False)
```
